256 devices in a mesh: gx: 8 (over y_hi, x), gy: 4 (over y_lo, core), ta: 8 (over z).
Axes of the slice: x: 4, y: 4 (y_hi: 2, y_lo: 2; y = y_hi * 2 + y_lo), z: 8, core: 2. Of those that a mesh axis runs over, the one named last changes fastest.
Arguments:
- displacement: float32 [3, 64, 32, 256], P(None, 'gx', 'gy'), may hold values from -3 to 3
- pressure: float32 [64, 32, 256], P('gx', 'gy'), may hold values from -6 to 6
- porosity: float32 [64, 32, 256], P('gx', 'gy'), may hold values from 0.1 to 0.3
- labels: int32 [64, 32, 256], P('gx', 'gy'), may hold values from 0 to 5
- ventricle_mask: int32 [64, 32, 256], P('gx', 'gy'), may hold values 0 or 1
- stiff_table: float32 [6], replicated, may hold values from 0.3 to 1.2
- perm_table: float32 [6], replicated, may hold values from 0.1 to 0.5
Outputs:
- slab_ends: float32 [8, 5, 64, 32, 256], P('ta', None, 'gx', 'gy')
The draws below stay inside these ranges and needn't reach their ends.
Inputs may be any that keep to these rules, and one draw needn't show every extreme that they name: `labels`: each label selects one row of the region tables.
All inputs are finite; a program needn't handle non-finite values. No bound on the sum of `ventricle_mask` on one device may be relied on, other than what follows from the above.
Results may differ from the reference program's by a relative error of at most 0.00002.
Values sent between devices are 32-bit elements; how exact they have to be, the bound alone decides.
No kernel may reach another device: no remote copies, remote signals or barrier semaphores. Data moves between devices by JAX's collectives and lax.ppermute only.
A program may use at most 64 MiB of HBM per device.

```python
import math
import jax
import jax.numpy as jnp

NZ = 256
FINE = 4
ITERS = 2
REGIONS = 6
NX = 64
NY = 32
SLABS = 8


def plant(values, own_key, smallest, largest):
    longest = values.shape.index(max(values.shape))
    spots = []
    for shift in (0, 1):
        where = [jax.random.randint(jax.random.fold_in(own_key, axis), (), 0, length) for axis, length in enumerate(values.shape)]
        where[longest] = (where[longest] + shift) % values.shape[longest]
        spots.append(tuple(where))
    return values.at[spots[0]].set(smallest).at[spots[1]].set(largest)


def block_levels(stream_key, extent, split, least, top_value):
    def one(position, parts):
        heights = jax.random.uniform(jax.random.fold_in(jax.random.fold_in(stream_key, 6), position), (parts,), jnp.float32, least / len(split), top_value / len(split))
        return jnp.repeat(jnp.exp(heights), extent[position] // parts).reshape((-1,) + (1,) * (len(extent) - position - 1))

    level = one(*split[0])
    for cut in split[1:]:
        level = level * one(*cut)
    return level


def gaussian(own_key, dims, deviation, reach, cuts=(), kind=jnp.bfloat16):
    drawn = jax.random.normal(own_key, dims, jnp.float32) * deviation
    if len(cuts) > 0:
        drawn = block_levels(own_key, dims, cuts, -0.22, 0.18) * drawn
    return jnp.clip(drawn, min=-reach, max=reach).astype(kind)


def setup_inputs(seed: int = 0) -> dict:
    arg_keys = jax.random.split(jax.random.key(seed), 8)
    return {
        "displacement": gaussian(arg_keys[0], (3, NX, NY, NZ), 0.5, 3.0, ((1, 8), (2, 4)), jnp.float32),
        "pressure": gaussian(arg_keys[1], (NX, NY, NZ), 1.0, 6.0, ((0, 8), (1, 4)), jnp.float32),
        "porosity": jnp.clip(0.1 + 0.20000001043081284 * jax.random.uniform(arg_keys[2], (NX, NY, NZ), jnp.float32) ** block_levels(arg_keys[2], (NX, NY, NZ), ((0, 8), (1, 4)), -0.2, 0.2), 0.1, 0.3),
        "labels": plant(jax.random.randint(arg_keys[3], (NX, NY, NZ), 0, REGIONS), jax.random.fold_in(arg_keys[3], 1), 0, REGIONS - 1).astype(jnp.int32),
        "ventricle_mask": plant((jax.random.randint(arg_keys[4], (NX, NY, NZ), 0, 6) < 1).astype(jnp.int32), jax.random.fold_in(arg_keys[4], 1), 0, 1),
        "stiff_table": jnp.clip(jnp.exp(jax.random.uniform(arg_keys[5], (REGIONS,), jnp.float32, math.log(0.3), math.log(1.2))), 0.3, 1.2),
        "perm_table": jnp.clip(jnp.exp(jax.random.uniform(arg_keys[6], (REGIONS,), jnp.float32, math.log(0.1), math.log(0.5))), 0.1, 0.5),
    }


coupling = 0.3
pressure_gain = 0.4
relax_rate = 0.5
stiffening = 2.0
porosity_ref = 0.2
fine_dt = 0.03


def lookup(labels, table):
    onehot = labels[None] == jnp.arange(table.shape[0], dtype=jnp.int32)[:, None, None, None]
    return jnp.sum(jnp.where(onehot, table[:, None, None, None], jnp.zeros((), table.dtype)), axis=0)


def statics(labels, ventricle_mask, stiff_table, perm_table):
    stiffness = lookup(labels, stiff_table)
    permbase = lookup(labels, perm_table)
    open_cells = 1.0 - ventricle_mask.astype(stiffness.dtype)
    inside = jnp.ones_like(stiffness)
    return jnp.stack([stiffness, permbase, open_cells, inside])


def advance(fields, coeffs, time_step):
    centre = fields[:, 1:-1, 1:-1]
    padded = jnp.pad(centre, ((0, 0), (0, 0), (0, 0), (1, 1)))
    upper = padded[..., 2:]
    lower = padded[..., :-2]
    east = fields[:, 2:, 1:-1]
    west = fields[:, :-2, 1:-1]
    north = fields[:, 1:-1, 2:]
    south = fields[:, 1:-1, :-2]
    stiffness = coeffs[0, 1:-1, 1:-1]
    open_cells = coeffs[2, 1:-1, 1:-1]
    inside = coeffs[3, 1:-1, 1:-1]
    conduct = coeffs[1] * jnp.exp(stiffening * (fields[4] - porosity_ref))
    conduct_mid = conduct[1:-1, 1:-1]
    conduct_pad = jnp.pad(conduct_mid, ((0, 0), (0, 0), (1, 1)))
    press_mid = centre[3]
    flux_sum = 0.5 * (conduct[2:, 1:-1] + conduct_mid) * (east[3] - press_mid)
    flux_sum = flux_sum + 0.5 * (conduct[:-2, 1:-1] + conduct_mid) * (west[3] - press_mid)
    flux_sum = flux_sum + 0.5 * (conduct[1:-1, 2:] + conduct_mid) * (north[3] - press_mid)
    flux_sum = flux_sum + 0.5 * (conduct[1:-1, :-2] + conduct_mid) * (south[3] - press_mid)
    flux_sum = flux_sum + 0.5 * (conduct_pad[:, :, 2:] + conduct_mid) * (upper[3] - press_mid)
    flux_sum = flux_sum + 0.5 * (conduct_pad[:, :, :-2] + conduct_mid) * (lower[3] - press_mid)
    displace_lap = east[0:3] + west[0:3] + north[0:3] + south[0:3] + upper[0:3] + lower[0:3] - 6.0 * centre[0:3]
    press_grad = 0.5 * jnp.stack([east[3] - west[3], north[3] - south[3], upper[3] - lower[3]])
    dilation = 0.5 * ((east[0] - west[0]) + (north[1] - south[1]) + (upper[2] - lower[2]))
    displace_new = inside * (centre[0:3] + time_step * (stiffness * displace_lap - coupling * press_grad))
    press_new = inside * open_cells * (press_mid + time_step * (flux_sum - pressure_gain * relax_rate * dilation))
    poro_new = inside * (centre[4] + time_step * relax_rate * (1.0 - centre[4]) * dilation)
    return jnp.concatenate([displace_new, press_new[None], poro_new[None]])


def pad_plane(fields):
    return jnp.pad(fields, ((0, 0), (1, 1), (1, 1), (0, 0)))


def reference(displacement, pressure, porosity, labels, ventricle_mask, stiff_table, perm_table):
    coeffs = pad_plane(statics(labels, ventricle_mask, stiff_table, perm_table))
    initial = jnp.concatenate([displacement, pressure[None], porosity[None]])

    def coarse(fields):
        return advance(pad_plane(fields), coeffs, fine_dt * FINE)

    def fine(fields):
        for _ in range(FINE):
            fields = advance(pad_plane(fields), coeffs, fine_dt)
        return fields

    begins = [initial]
    coarse_old = []
    for slab in range(SLABS):
        handed = coarse(begins[-1])
        coarse_old.append(handed)
        if slab + 1 < SLABS:
            begins.append(handed)
    ends = []
    for _ in range(ITERS):
        fine_outs = [fine(begin_state) for begin_state in begins]
        new_begins = [initial]
        new_coarse = []
        ends = []
        for slab in range(SLABS):
            handed = coarse(new_begins[slab])
            new_coarse.append(handed)
            end_state = handed + (fine_outs[slab] - coarse_old[slab])
            ends.append(end_state)
            if slab + 1 < SLABS:
                new_begins.append(end_state)
        begins = new_begins
        coarse_old = new_coarse
    return jnp.stack(ends)
```

```python
import math

import jax
import jax.numpy as jnp
from jax import lax
from jax.experimental import pallas as pl
from jax.experimental.pallas import tpu as pltpu
from jax.sharding import PartitionSpec as P

FINE = 4
coupling = 0.3
pressure_gain = 0.4
relax_rate = 0.5
stiffening = 2.0
porosity_ref = 0.2
fine_dt = 0.03

F32 = jnp.float32
INTERPRET = False

DEPTH = 15
CHUNK = 104
PLANE = 32
FIELD = 16 * PLANE
SLOT = 6 * FIELD
A0, B0, T0, SLOTS = 0, 8, 17, 19
LAST = DEPTH - 1


def lanes():
    return lax.broadcasted_iota(jnp.int32, (8, 128), 1)


def exchange_bits(v):
    lane = lanes()
    for b in range(3):
        high = ((lane >> (3 + b)) & 1) == 1
        step = 8 << b
        new = list(v)
        for i in range(8):
            if not (i >> b) & 1:
                j = i | (1 << b)
                new[i] = jnp.where(high, pltpu.roll(v[j], step, 1), v[i])
                new[j] = jnp.where(high, v[j], pltpu.roll(v[i], 128 - step, 1))
        v = new
    return v


def pack_kernel(ta_ref, disp, pres, poro, lab, mask, out, flat, big, win, rev):
    ta = ta_ref[0]
    for f in range(7):
        field = disp[f] if f < 3 else (pres, poro, lab, mask)[f - 3][...].astype(F32)
        for h in range(2):
            flat[(f * 2 + h) * 64 : (f * 2 + h + 1) * 64, :] = field[:, h * 128 : (h + 1) * 128]

    def rows(f, h):
        return [flat[pl.ds((f * 2 + h) * 64 + y, 8, stride=8), :] for y in range(8)]

    big[:, 0:16, :] = jnp.zeros((4, 16, 128), F32)
    big[:, 272:288, :] = jnp.zeros((4, 16, 128), F32)
    for t in range(4):
        for h in range(2):
            pair = jnp.concatenate(rows(2 * t, h) + rows(min(2 * t + 1, 6), h), axis=0)
            big[t, 16 + h * 128 : 144 + h * 128, :] = pair.T
        win[t, :, :] = big[t, pl.ds(pl.multiple_of(ta * 32, 32), 64), :]
        for i in range(64):
            rev[t, i : i + 1, :] = win[t, 63 - i : 64 - i, :]
        win[t + 4, :, :] = pltpu.roll(win[t, :, :], 64, 1)
        rev[t + 4, :, :] = pltpu.roll(rev[t, :, :], 64, 1)
    low = lax.broadcasted_iota(jnp.int32, (15, 128), 1) < 64
    for g in range(32):
        for f in range(7):
            t = f // 2
            first = win[t + 4 * (f % 2), g + 2 : g + 17, :]
            second = rev[t + 4 * (1 - f % 2), 32 - g : 47 - g, :]
            both = jnp.where(low, first, second)
            if f < 5:
                out[g * CHUNK + f * 15 : g * CHUNK + f * 15 + 15, :] = both
            else:
                at = g * CHUNK + 75 + (f - 5) * 14
                out[at : at + 14, :] = both[1:, :]
        out[g * CHUNK + 103 : g * CHUNK + 104, :] = jnp.zeros((1, 128), F32)


def main_kernel(c_ref, stiff_tab, perm_tab, recv, out, st, raw, co, inside, ends):
    lane = lanes()
    row = lax.broadcasted_iota(jnp.int32, (8, 128), 0)
    half0 = lane < 64
    x = lane & 63
    has_e, has_w = x < 63, x > 0
    has_n, has_s = row < 7, row > 0
    zero = jnp.zeros((8, 128), F32)

    def tile(start):
        return pl.ds(pl.multiple_of(start, 8), 8)

    def base(slot, f, zl):
        return slot * SLOT + f * FIELD + zl * PLANE

    def relayout(group, carry):
        for gy in range(4):
            v = [recv[tile((gx * 4 + gy) * CHUNK + group * 8), :] for gx in range(8)]
            v = exchange_bits(v)
            for yq in range(8):
                place = (yq % 4) * 8 + 2 * gy + yq // 4
                raw[pl.ds(group * (8 * PLANE) + place, 8, stride=PLANE), :] = v[yq]
        return carry

    lax.fori_loop(0, CHUNK // 8, relayout, 0)

    c = c_ref[0]
    scale = stiffening * math.log2(math.e)

    def conduct(perm, phi):
        return perm * jnp.exp2((phi - porosity_ref) * scale)

    def coefficients(zl, carry):
        z = jnp.where(half0, c - 14 + zl, c + 15 - zl)
        m = jnp.where((z >= 0) & (z < 256), 1.0, 0.0).astype(F32)
        inside[tile(zl * 8), :] = m
        for yl in range(4):
            label = raw[tile((74 + zl) * PLANE + 8 * yl), :]
            drain = raw[tile((88 + zl) * PLANE + 8 * yl), :]
            stiff, perm = zero, zero
            for i in range(6):
                hit = label == float(i)
                stiff = jnp.where(hit, stiff_tab[i], stiff)
                perm = jnp.where(hit, perm_tab[i], perm)
            stiff = stiff * m
            fine_a = stiff * fine_dt
            coarse_a = stiff * (fine_dt * FINE)
            values = (
                fine_a,
                1.0 - 6.0 * fine_a,
                coarse_a,
                1.0 - 6.0 * coarse_a,
                (1.0 - drain) * m,
                perm * m * (0.5 * fine_dt),
            )
            for i, value in enumerate(values):
                co[tile((i * DEPTH + zl) * PLANE + 8 * yl), :] = value
        return carry

    lax.fori_loop(1, DEPTH, coefficients, 0)
    for yl in range(4):
        co[tile(5 * DEPTH * PLANE + 8 * yl), :] = zero

    sign = jnp.where(half0, 1.0, -1.0).astype(F32)

    def put(slot, zl, yl, vals, k=None, last=False):
        for f in range(5):
            st[tile(base(slot, f, zl) + 8 * yl), :] = vals[f]
        if k is not None:
            st[tile(base(slot, 5, zl) + 8 * yl), :] = k
            if last:
                for f, v in ((0, vals[0]), (1, vals[1]), (2, -vals[2]), (3, vals[3]), (5, k)):
                    st[tile(base(slot, f, DEPTH) + 8 * yl), :] = pltpu.roll(v, 64, 1)

    def get(slot, f, zl, yl):
        return st[tile(base(slot, f, zl) + 8 * yl), :]

    def coef(i, zl, yl):
        return co[tile((i * DEPTH + zl) * PLANE + 8 * yl), :]

    def sweep(first, body):
        def step(zl, carry):
            body(zl, False)
            return carry

        lax.fori_loop(first, LAST, step, 0)
        body(LAST, True)

    def stage_start(zl, last):
        for yl in range(4):
            vals = [raw[tile((f * 15 + zl) * PLANE + 8 * yl), :] for f in range(5)]
            vals[2] = vals[2] * sign
            put(A0, zl, yl, vals, conduct(coef(5, zl, yl), vals[4]), last)

    sweep(0, stage_start)

    def advance(src, zl, fine, emit):
        dt = fine_dt if fine else fine_dt * FINE
        at = base(src, 0, zl)

        def load(f, yl, dz=0):
            return st[tile(at + f * FIELD + dz * PLANE + 8 * yl), :]

        m = inside[tile(zl * 8), :]
        grad_c = m * (dt * coupling * 0.5)
        poro_c = m * (dt * relax_rate * 0.5)
        cen = {f: [load(f, yl) for yl in range(4)] for f in (0, 1, 2, 3, 5)}
        up = {f: jnp.where(has_n, pltpu.roll(cen[f][0], 7, 0), 0.0) for f in cen}
        dn = {f: jnp.where(has_s, pltpu.roll(cen[f][3], 1, 0), 0.0) for f in cen}
        face = (dn[5] + cen[5][0]) * (cen[3][0] - dn[3])
        for yl in range(4):
            mid = {f: cen[f][yl] for f in cen}
            e = {f: jnp.where(has_e, pltpu.roll(mid[f], 127, 1), 0.0) for f in cen}
            w = {f: jnp.where(has_w, pltpu.roll(mid[f], 1, 1), 0.0) for f in cen}
            n = {f: cen[f][yl + 1] if yl < 3 else up[f] for f in cen}
            s = {f: cen[f][yl - 1] if yl > 0 else dn[f] for f in cen}
            i = {f: load(f, yl, 1) for f in cen}
            o = {f: load(f, yl, -1) for f in cen}
            p, k = mid[3], mid[5]
            next_face = (n[5] + k) * (n[3] - p)
            flux = next_face - face
            face = next_face
            for side in (e, w, i, o):
                flux = flux + (side[5] + k) * (side[3] - p)
            dil = (e[0] - w[0]) + (n[1] - s[1]) + (i[2] - o[2])
            grads = (e[3] - w[3], n[3] - s[3], i[3] - o[3])
            a = coef(0 if fine else 2, zl, yl)
            a6 = coef(1 if fine else 3, zl, yl)
            new = []
            for f in range(3):
                around = (e[f] + w[f]) + (n[f] + s[f]) + (i[f] + o[f])
                new.append(a * around + a6 * mid[f] - grad_c * grads[f])
            if not fine:
                flux = flux * float(FINE)
            gain = dt * pressure_gain * relax_rate * 0.5
            new.append(coef(4, zl, yl) * (p + (flux - gain * dil)))
            phi = load(4, yl)
            new.append(phi + (poro_c * dil) * (1.0 - phi))
            emit(yl, new)

    def plain(src, dst, first, fine):
        def body(zl, last):
            def emit(yl, new):
                put(dst, zl, yl, new, conduct(coef(5, zl, yl), new[4]), last)

            advance(src, zl, fine, emit)

        sweep(first, body)

    def minus(src, sub, dst, first):
        def body(zl, last):
            def emit(yl, new):
                put(dst, zl, yl, [new[f] - get(sub, f, zl, yl) for f in range(5)])

            advance(src, zl, True, emit)

        sweep(first, body)

    def plus(src, cor, dst, first, keep):
        def body(zl, last):
            def emit(yl, new):
                vals = [new[f] + get(cor, f, zl, yl) for f in range(5)]
                if keep:
                    put(cor, zl, yl, new)
                put(dst, zl, yl, vals, conduct(coef(5, zl, yl), vals[4]), last)

            advance(src, zl, False, emit)

        sweep(first, body)

    def fine_all(source, start, count):
        def slab(j, carry):
            def inner(s, carry):
                src = jnp.where(s == 0, source + j, T0 + ((s + 1) & 1))
                plain(src, T0 + (s & 1), start + j + s, True)
                return carry

            lax.fori_loop(0, FINE - 1, inner, 0)
            minus(T0, A0 + j + 1, A0 + j, start + j + FINE - 1)

            @pl.when(j == 0)
            def _():
                for yl in range(4):
                    put(B0, LAST, yl, [get(B0 + 1, f, LAST, yl) for f in range(5)])

                def body(zl, last):
                    for yl in range(4):
                        vals = [get(A0 + 1, f, zl, yl) + get(A0, f, zl, yl) for f in range(5)]
                        put(B0 + 1, zl, yl, vals, conduct(coef(5, zl, yl), vals[4]), last)

                sweep(start + FINE - 1, body)

            return carry

        lax.fori_loop(0, count, slab, 0)

    def chain0(k, carry):
        plain(A0 + k, A0 + k + 1, jnp.where(k == 6, 10, k + 1), False)
        return carry

    lax.fori_loop(0, 7, chain0, 0)
    fine_all(A0, 1, 7)

    def chain1(k, carry):
        plus(B0 + k, A0 + k, B0 + k + 1, jnp.where(k == 7, 14, k + 4), True)
        return carry

    lax.fori_loop(1, 8, chain1, 0)
    fine_all(B0 + 1, 5, 7)

    def chain2(k, carry):
        plus(B0 + k - 1, A0 + k - 1, B0 + k, k + 7, False)
        return carry

    lax.fori_loop(2, 8, chain2, 0)

    for t in range(3):
        for gy in range(4):
            v = []
            for yq in range(8):
                place = (yq % 4) * 8 + 2 * gy + yq // 4
                first = st[pl.ds(B0 * SLOT + 2 * t * FIELD + LAST * PLANE + place, 8, stride=SLOT), :]
                if t < 2:
                    second = st[pl.ds(B0 * SLOT + (2 * t + 1) * FIELD + LAST * PLANE + place, 8, stride=SLOT), :]
                    second = pltpu.roll(second, 64, 1)
                else:
                    second = zero
                v.append(jnp.where(half0, first, second))
            v = exchange_bits(v)
            for gx in range(8):
                ends[pl.ds(t * 256 + gx * 4 + gy, 8, stride=32), :] = v[gx]
        out[:, t * 128 : (t + 1) * 128] = ends[t * 256 : (t + 1) * 256, :]


def unpack_kernel(recv, out, turned):
    for t in range(3):
        for h in range(2):
            block = recv[h * 128 : (h + 1) * 128, t * 128 : (t + 1) * 128]
            turned[h * 384 + t * 128 : h * 384 + (t + 1) * 128, :] = block.T
    for f in range(5):
        for x in range(8):
            for h in range(2):
                at = (f * 8 + x) * 8
                out[at : at + 8, h * 128 : (h + 1) * 128] = turned[pl.ds(h * 384 + f * 64 + x, 8, stride=8), :]


def vmem(n=None):
    return pl.BlockSpec(memory_space=pltpu.VMEM)


def smem():
    return pl.BlockSpec(memory_space=pltpu.SMEM)


def pack(ta, disp, pres, poro, lab, mask):
    return pl.pallas_call(
        pack_kernel,
        out_shape=jax.ShapeDtypeStruct((32 * CHUNK, 128), F32),
        in_specs=[smem()] + [vmem()] * 5,
        out_specs=vmem(),
        scratch_shapes=[
            pltpu.VMEM((7 * 2 * 64, 128), F32),
            pltpu.VMEM((4, 288, 128), F32),
            pltpu.VMEM((8, 64, 128), F32),
            pltpu.VMEM((8, 64, 128), F32),
        ],
        interpret=INTERPRET,
        name="pack",
    )(ta, disp, pres, poro, lab, mask)


def compute(c, stiff_table, perm_table, recv):
    return pl.pallas_call(
        main_kernel,
        out_shape=jax.ShapeDtypeStruct((256, 384), F32),
        in_specs=[smem(), smem(), smem(), vmem()],
        out_specs=vmem(),
        scratch_shapes=[
            pltpu.VMEM((SLOTS * SLOT, 128), F32),
            pltpu.VMEM((CHUNK * PLANE, 128), F32),
            pltpu.VMEM((6 * DEPTH * PLANE, 128), F32),
            pltpu.VMEM((DEPTH * 8, 128), F32),
            pltpu.VMEM((3 * 256, 128), F32),
        ],
        compiler_params=pltpu.CompilerParams(vmem_limit_bytes=48 << 20),
        interpret=INTERPRET,
        name="parareal",
    )(c, stiff_table, perm_table, recv)


def unpack(recv):
    return pl.pallas_call(
        unpack_kernel,
        out_shape=jax.ShapeDtypeStruct((320, 256), F32),
        in_specs=[vmem()],
        out_specs=vmem(),
        scratch_shapes=[pltpu.VMEM((768, 128), F32)],
        interpret=INTERPRET,
        name="unpack",
    )(recv)


def shards(displacement, pressure, porosity, labels, ventricle_mask, stiff_table, perm_table):
    ta = lax.axis_index("ta").astype(jnp.int32)
    plane = ta * 32 + lax.axis_index("gx") * 4 + lax.axis_index("gy")
    flat = lambda a: a.reshape(a.shape[:-3] + (64, 256))
    sent = pack(
        ta.reshape(1), flat(displacement), flat(pressure), flat(porosity), flat(labels), flat(ventricle_mask)
    )
    got = lax.all_to_all(sent.reshape(32, CHUNK, 128), ("gx", "gy"), 0, 0, tiled=True)
    ends = compute(plane.astype(jnp.int32).reshape(1), stiff_table, perm_table, got.reshape(32 * CHUNK, 128))
    mine = lax.all_to_all(ends, ("ta", "gx", "gy"), 0, 0, tiled=True)
    return unpack(mine).reshape(1, 5, 8, 8, 256)


def solution(mesh):
    placed = (
        P(None, "gx", "gy", None),
        P("gx", "gy", None),
        P("gx", "gy", None),
        P("gx", "gy", None),
        P("gx", "gy", None),
        P(),
        P(),
    )
    return jax.shard_map(
        shards,
        mesh=mesh,
        in_specs=placed,
        out_specs=P("ta", None, "gx", "gy", None),
        check_vma=False,
    )
```

```python
import math

import jax
import jax.numpy as jnp
from jax import lax
from jax.experimental import pallas as pl
from jax.experimental.pallas import tpu as pltpu
from jax.sharding import PartitionSpec as P

FINE = 4
coupling = 0.3
pressure_gain = 0.4
relax_rate = 0.5
stiffening = 2.0
porosity_ref = 0.2
fine_dt = 0.03

F32 = jnp.float32
INTERPRET = False

REACH = 18
ROWS = 128
PLANE = 24
FIELD = 19 * PLANE
SLOT = 6 * FIELD
PAD = 8 + 4 * PLANE
SHARP = stiffening * math.log2(math.e)
U_SCALE = fine_dt * relax_rate * 0.5
P_SCALE = U_SCALE * fine_dt * coupling * 0.5
GAIN = fine_dt * pressure_gain * relax_rate * 0.5 * P_SCALE / U_SCALE
MOVED = (0, 1, 2, 3, 5)


def lanes():
    return lax.broadcasted_iota(jnp.int32, (8, 128), 1)


def exchange_bits(v):
    lane = lanes()
    for b in range(2):
        high = ((lane >> (3 + b)) & 1) == 1
        step = 8 << b
        new = list(v)
        for i in range(4):
            if not (i >> b) & 1:
                j = i | (1 << b)
                new[i] = jnp.where(high, pltpu.roll(v[j], step, 1), v[i])
                new[j] = jnp.where(high, v[j], pltpu.roll(v[i], 128 - step, 1))
        v = new
    return v


def pack_kernel(ta_ref, disp, pres, poro, lab, mask, out, flat, big, win, rev):
    ta = ta_ref[0]
    zero = jnp.zeros((16, 128), F32)
    for f in range(7):
        field = disp[f] if f < 3 else (pres, poro, lab, mask)[f - 3][...].astype(F32)
        for h in range(2):
            flat[(f * 2 + h) * 64 : (f * 2 + h + 1) * 64, :] = field[:, h * 128 : (h + 1) * 128]

    def rows(f, h, xf):
        for xi in range(4):
            at = (f * 2 + h) * 64 + (4 + xi if xf else 3 - xi) * 8
            yield flat[at : at + 8, :]

    for t in range(4):
        one, two = 2 * t, min(2 * t + 1, 6)
        big[t * 288 : t * 288 + 16, :] = zero
        big[t * 288 + 272 : t * 288 + 288, :] = zero
        for h in range(2):
            parts = [part for xf in range(2) for f in (one, two) for part in rows(f, h, xf)]
            at = t * 288 + 16 + h * 128
            big[at : at + 128, :] = jnp.concatenate(parts, axis=0).T
        win[t * 64 : t * 64 + 64, :] = big[pl.ds(pl.multiple_of(t * 288 + ta * 32, 32), 64), :]
        for i in range(64):
            rev[t * 64 + i : t * 64 + i + 1, :] = win[t * 64 + 63 - i : t * 64 + 64 - i, :]
        win[256 + t * 64 : 320 + t * 64, :] = pltpu.roll(win[t * 64 : t * 64 + 64, :], 32, 1)
        rev[256 + t * 64 : 320 + t * 64, :] = pltpu.roll(rev[t * 64 : t * 64 + 64, :], 96, 1)
    near = (lax.broadcasted_iota(jnp.int32, (REACH, 128), 1) & 32) == 0
    for g in range(4):
        for f in range(7):
            t, odd = f // 2, f % 2
            low = 256 * odd + t * 64 + 44 - 8 * g
            high = 256 * (1 - odd) + t * 64 + 20 + 8 * g
            both = jnp.where(near, rev[low : low + REACH, :], win[high : high + REACH, :])
            out[g * ROWS + f * REACH : g * ROWS + (f + 1) * REACH, :] = both
        out[g * ROWS + 126 : g * ROWS + 128, :] = jnp.zeros((2, 128), F32)


def fold_kernel(recv, own, down, up):
    half0 = lanes() < 64

    def group(r, carry):
        def at(i):
            return pl.ds(pl.multiple_of(i * ROWS + r * 8, 8), 8)

        v = exchange_bits([recv[at(gy), :] for gy in range(4)])
        for i in range(4):
            own[at(i), :] = v[i]
        for i in range(2):
            down[at(i), :] = v[i]
            up[at(i), :] = v[i]
        down[at(2), :] = jnp.where(half0, v[2], pltpu.roll(v[3], 64, 1))
        up[at(2), :] = jnp.where(half0, pltpu.roll(v[3], 64, 1), v[2])
        return carry

    lax.fori_loop(0, ROWS // 8, group, 0)


def main_kernel(pos_ref, stiff_tab, cond_tab, own, east, west, east2, west2, out, a_st, b_st, c_st, t0, t1, raw, co, turn):
    lane = lanes()
    row = lax.broadcasted_iota(jnp.int32, (8, 128), 0)
    half0 = lane < 64
    near_z = (lane & 32) == 0
    y = lane & 31
    has_n, has_s = y < 31, y > 0
    zero = jnp.zeros((8, 128), F32)

    def swap_x(v):
        return pltpu.roll(v, 64, 1)

    def swap_z(v):
        return jnp.where(near_z, pltpu.roll(v, 96, 1), pltpu.roll(v, 32, 1))

    def tile(start):
        return pl.ds(pl.multiple_of(start, 8), 8)

    def spread(r, carry):
        def get(ref, i):
            return ref[tile(i * ROWS + r * 8), :]

        def place(xi, v):
            raw[pl.ds(r * (8 * PLANE) + xi, 8, stride=PLANE), :] = v

        for i in range(4):
            place(i, get(own, i))
            place(4 + i, swap_x(jnp.where(half0, get(east, 3 - i), get(west, 3 - i))))
            place(8 + i, jnp.where(half0, get(west, i), get(east, i)))
        for i in range(2):
            place(14 + i, swap_x(jnp.where(half0, get(east2, 1 - i), get(west2, 1 - i))))
            place(16 + i, jnp.where(half0, get(west2, i), get(east2, i)))
        e, w = get(east2, 2), get(west2, 2)
        place(13, swap_x(jnp.where(half0, e, w)))
        place(12, jnp.where(half0, w, e))
        for i in range(6):
            place(18 + i, zero)
        return carry

    lax.fori_loop(0, ROWS // 8, spread, 0)

    x0, z0 = pos_ref[0], pos_ref[1]

    def coefficients(zi, carry):
        z = jnp.where(near_z, z0 + 3 - zi, z0 + 4 + zi)
        in_z = (z >= 0) & (z < 256)
        for b in range(3):
            xi = row + 8 * b
            x = jnp.where(half0, x0 + 3 - xi, x0 + 4 + xi)
            here = in_z & (x >= 0) & (x < 64)
            label = raw[tile((5 * REACH + zi) * PLANE + 8 * b), :]
            drain = raw[tile((6 * REACH + zi) * PLANE + 8 * b), :]
            stiff, cond = zero, zero
            for i in range(6):
                hit = label == float(i)
                stiff = jnp.where(hit, stiff_tab[i], stiff)
                cond = jnp.where(hit, cond_tab[i], cond)
            stiff = jnp.where(here, stiff, 0.0)
            fine_a = stiff * fine_dt
            coarse_a = stiff * (fine_dt * FINE)
            values = (
                fine_a,
                1.0 - 6.0 * fine_a,
                coarse_a,
                1.0 - 6.0 * coarse_a,
                jnp.where(here, 1.0 - drain, 0.0),
                jnp.where(here, cond, -1.0e30),
                jnp.where(here, 1.0, 0.0).astype(F32),
            )
            for i, value in enumerate(values):
                co[tile(i * FIELD + (zi + 1) * PLANE + 8 + 8 * b), :] = value
        return carry

    lax.fori_loop(0, REACH, coefficients, 0)

    sign_x = jnp.where(half0, -U_SCALE, U_SCALE).astype(F32)
    sign_z = jnp.where(near_z, -U_SCALE, U_SCALE).astype(F32)

    def where_of(slot, zi, b0=0):
        return pl.multiple_of(slot * SLOT + (zi + 1) * PLANE + 8 + 8 * b0, 8)

    def load(ref, at, f, off=0):
        return ref[pl.ds(at + (f * FIELD + off), 8), :]

    def coef(at, i, off):
        return co[pl.ds(at + (i * FIELD + off), 8), :]

    def put(ref, at, off, vals, k=None):
        for f in range(5):
            ref[pl.ds(at + (f * FIELD + off), 8), :] = vals[f]
        if k is not None:
            ref[pl.ds(at + (5 * FIELD + off), 8), :] = k

    def conduct(ca, off, psi):
        return jnp.exp2(coef(ca, 5, off) - psi)

    def begin(zi, carry):
        at, ca = where_of(0, zi), where_of(0, zi)
        for b in range(3):
            vals = [raw[tile((f * REACH + zi) * PLANE + 8 * b), :] for f in range(5)]
            vals[0] = vals[0] * sign_x
            vals[1] = vals[1] * U_SCALE
            vals[2] = vals[2] * sign_z
            vals[3] = vals[3] * P_SCALE
            vals[4] = (1.0 - vals[4]) * SHARP
            k = conduct(ca, 8 * b, vals[4])
            for ref in (a_st, t1):
                put(ref, at, 8 * b, vals, k)
        return carry

    lax.fori_loop(0, REACH, begin, 0)

    def prepare(ref, at):
        for d in range(2):
            for b in range(2):
                for i, f in enumerate(MOVED):
                    v = load(ref, at, f, d * PLANE + 8 * b)
                    to = ((d * 2 + b) * 5 + i) * 16
                    turn[to : to + 8, :] = jnp.where(has_n, pltpu.roll(v, 127, 1), 0.0)
                    turn[to + 8 : to + 16, :] = jnp.where(has_s, pltpu.roll(v, 1, 1), 0.0)

    def advance(ref, slot, radius, fine, emit):
        units = (radius + 5) // 2
        passes = jnp.where(radius > 12, 2, 1)

        def unit(at, ca, carry, more):
            carry = list(carry)
            for d in range(2):
                for b in range(2):
                    off = d * PLANE + 8 * b
                    mid = {f: load(ref, at, f, off) for f in MOVED}
                    e = {f: load(ref, at, f, off + 1) for f in MOVED}
                    w = {f: load(ref, at, f, off - 1) for f in MOVED}
                    i = {f: load(ref, at, f, off + PLANE) for f in MOVED}
                    o = {f: load(ref, at, f, off - PLANE) for f in (0, 1, 2, 3)}
                    n, s = {}, {}
                    for j, f in enumerate(MOVED):
                        to = ((d * 2 + b) * 5 + j) * 16
                        n[f] = turn[to : to + 8, :]
                        s[f] = turn[to + 8 : to + 16, :]
                    p, k = mid[3], mid[5]
                    face = (i[5] + k) * (i[3] - p)
                    flux = face - carry[b]
                    carry[b] = face
                    for side in (e, w, n, s):
                        flux = flux + (side[5] + k) * (side[3] - p)
                    dil = (e[0] - w[0]) + (n[1] - s[1]) + (i[2] - o[2])
                    m = coef(ca, 6, off)
                    grads = [e[3] - w[3], n[3] - s[3], i[3] - o[3]]
                    gain = GAIN
                    if not fine:
                        m = m * float(FINE)
                        grads[1] = grads[1] * float(FINE)
                        flux = flux * float(FINE)
                        gain = GAIN * FINE
                    grads[0] = grads[0] * m
                    grads[2] = grads[2] * m
                    a = coef(ca, 0 if fine else 2, off)
                    a6 = coef(ca, 1 if fine else 3, off)
                    new = []
                    for f in range(3):
                        around = (e[f] + w[f]) + (n[f] + s[f]) + (i[f] + o[f])
                        new.append(a * around + a6 * mid[f] - grads[f])
                    new.append(coef(ca, 4, off) * (p + (flux - gain * dil)))
                    psi = load(ref, at, 4, off)
                    new.append(psi * (1.0 - (dil if fine else dil * float(FINE))))
                    emit(at - slot * SLOT, ca, off, new)
            if more:
                prepare(ref, pl.multiple_of(at + 2 * PLANE, 8))
            return tuple(carry)

        start = where_of(slot, 0)

        def ghost_x(f, zi):
            row0 = start + (f * FIELD + zi * PLANE)
            v = ref[pl.ds(row0, 8, stride=PLANE), :]
            ref[pl.ds(row0 - 1, 8, stride=PLANE), :] = swap_x(-v if f == 0 else v)

        def ghost_z(f, b):
            v = load(ref, start, f, 8 * b)
            v = swap_z(-v if f == 2 else v)
            ref[pl.ds(start + (f * FIELD + 8 * b - PLANE), 8), :] = v
            return v

        @pl.when(radius > 12)
        def _():
            for f in MOVED:
                ghost_z(f, 2)
                ghost_x(f, 10)

        def one_pass(j, c):
            b0 = passes - 1 - j
            at, ca = where_of(slot, 0, b0), where_of(0, 0, b0)
            for f in MOVED:
                ghost_x(f, 0)
                ghost_x(f, 8)
            for f in (0, 1, 2):
                for b in range(2):
                    ghost_z(f, b)
            carry = []
            for b in range(2):
                ghost_z(3, b)
                ghost_z(5, b)
            prepare(ref, at)
            for b in range(2):
                k0, k1 = load(ref, at, 5, 8 * b - PLANE), load(ref, at, 5, 8 * b)
                p0, p1 = load(ref, at, 3, 8 * b - PLANE), load(ref, at, 3, 8 * b)
                carry.append((k0 + k1) * (p1 - p0))

            def step(u, carry):
                shift = u * (2 * PLANE)
                return unit(pl.multiple_of(at + shift, 8), pl.multiple_of(ca + shift, 8), carry, True)

            carry = lax.fori_loop(0, units - 1, step, tuple(carry))
            shift = (units - 1) * (2 * PLANE)
            unit(pl.multiple_of(at + shift, 8), pl.multiple_of(ca + shift, 8), carry, False)
            return c

        lax.fori_loop(0, passes, one_pass, 0)

    def slot_at(slot, at):
        return pl.multiple_of(slot * SLOT + at, 8)

    def plain(src, slot, radius, fine, *targets):
        def emit(at, ca, off, new):
            k = conduct(ca, off, new[4])
            for ref, to in targets:
                put(ref, slot_at(to, at), off, new, k)

        advance(src, slot, radius, fine, emit)

    def minus(src, slot, radius, sub, to):
        def emit(at, ca, off, new):
            old = slot_at(sub, at)
            put(c_st, slot_at(to, at), off, [new[f] - load(a_st, old, f, off) for f in range(5)])

        advance(src, slot, radius, True, emit)

    def plus(src, radius, cor, keep, *targets):
        def emit(at, ca, off, new):
            if keep is not None:
                put(a_st, slot_at(keep, at), off, new)
            if targets:
                old = slot_at(cor, at)
                vals = [new[f] + load(c_st, old, f, off) for f in range(5)]
                k = conduct(ca, off, vals[4])
                for ref, to in targets:
                    put(ref, slot_at(to, at), off, vals, k)

        advance(src, 0, radius, False, emit)

    def fine_all(source, base, start):
        def slab(j, carry):
            plain(source, base + j, start - j, True, (t0, 0))
            plain(t0, 0, start - 1 - j, True, (t1, 0))
            plain(t1, 0, start - 2 - j, True, (t0, 0))
            minus(t0, 0, start - 3 - j, j + 1, j)

            @pl.when(j == 0)
            def _():
                for zi in range(4):
                    put(b_st, where_of(0, zi), 0, [load(b_st, where_of(1, zi), f) for f in range(5)])

                def body(zi, carry):
                    at = where_of(0, zi)
                    for b in range(2):
                        off = 8 * b
                        vals = [load(a_st, slot_at(1, at), f, off) + load(c_st, at, f, off) for f in range(5)]
                        put(b_st, slot_at(1, at), off, vals, conduct(at, off, vals[4]))
                    return carry

                lax.fori_loop(0, start + 1, body, 0)

            return carry

        lax.fori_loop(0, 7, slab, 0)

    def restart():
        def step(i, carry):
            for j in range(9):
                at = i * 72 + 8 * j
                t1[tile(at), :] = b_st[tile(SLOT + at), :]
            return carry

        lax.fori_loop(0, SLOT // 72, step, 0)

    def chain0(i, carry):
        k = 2 * i
        plain(t1, 0, 13 - k, False, (t0, 0), (a_st, k + 1))
        plain(t0, 0, 12 - k, False, (t1, 0), (a_st, k + 2))
        return carry

    lax.fori_loop(0, 3, chain0, 0)
    plain(t1, 0, jnp.int32(4), False, (a_st, 7))
    fine_all(a_st, 0, 13)
    restart()

    def chain1(i, carry):
        k = 2 * i + 1
        plus(t1, 10 - k, k, k, (t0, 0), (b_st, k + 1))
        plus(t0, 9 - k, k + 1, k + 1, (t1, 0), (b_st, k + 2))
        return carry

    lax.fori_loop(0, 3, chain1, 0)
    plus(t1, jnp.int32(0), None, 7)
    fine_all(b_st, 1, 9)
    restart()

    def chain2(i, carry):
        k = 2 * i + 2
        plus(t1, 7 - k, k - 1, None, (t0, 0), (b_st, k))
        plus(t0, 6 - k, k, None, (t1, 0), (b_st, k + 1))
        return carry

    lax.fori_loop(0, 3, chain2, 0)

    unsign_x = jnp.where(half0, -1.0 / U_SCALE, 1.0 / U_SCALE).astype(F32)
    unsign_z = jnp.where(near_z, -1.0 / U_SCALE, 1.0 / U_SCALE).astype(F32)
    for f in range(5):
        for zi in range(4):
            v = []
            for xi in range(4):
                e = b_st[pl.ds(f * FIELD + (zi + 1) * PLANE + 8 + xi, 8, stride=SLOT), :]
                if f == 4:
                    e = 1.0 - e * (1.0 / SHARP)
                else:
                    e = e * (unsign_x, 1.0 / U_SCALE, unsign_z, 1.0 / P_SCALE)[f]
                v.append(e)
            v = exchange_bits(v)
            for gy in range(4):
                out[pl.ds(gy * 24 + f * 4 + zi, 8, stride=96), :] = v[gy]
    for i in range(32):
        out[i * 24 + 20 : i * 24 + 24, :] = jnp.zeros((4, 128), F32)


def unpack_kernel(recv, out, rows):
    near_z = (lanes() & 32) == 0
    for t in range(3):
        for zi in range(4):
            for g in range(4):
                one = recv[pl.ds(g * 192 + 2 * t * 4 + zi, 8, stride=24), :]
                two = recv[pl.ds(g * 192 + min(2 * t + 1, 4) * 4 + zi, 8, stride=24), :]
                low = jnp.where(near_z, one, pltpu.roll(two, 32, 1))
                high = jnp.where(near_z, pltpu.roll(one, 96, 1), two)
                rows[pl.ds(t * 256 + g * 64 + 3 - zi, 8, stride=8), :] = low
                rows[pl.ds(t * 256 + g * 64 + 4 + zi, 8, stride=8), :] = high
        for h in range(2):
            block = rows[t * 256 + h * 128 : t * 256 + (h + 1) * 128, :].T
            for i in range(1 if t == 2 else 2):
                for xf in range(2):
                    for xi in range(4):
                        at = ((2 * t + i) * 8 + (4 + xi if xf else 3 - xi)) * 8
                        source = xf * 64 + i * 32 + xi * 8
                        out[at : at + 8, h * 128 : (h + 1) * 128] = block[source : source + 8, :]


def vmem():
    return pl.BlockSpec(memory_space=pltpu.VMEM)


def smem():
    return pl.BlockSpec(memory_space=pltpu.SMEM)


def scratch(rows):
    return pltpu.VMEM((rows, 128), F32)


def shaped(rows, width=128):
    return jax.ShapeDtypeStruct((rows, width), F32)


def pack(ta, *fields):
    return pl.pallas_call(
        pack_kernel,
        out_shape=shaped(4 * ROWS),
        in_specs=[smem()] + [vmem()] * 5,
        out_specs=vmem(),
        scratch_shapes=[scratch(896), scratch(1152), scratch(512), scratch(512)],
        interpret=INTERPRET,
        name="pack",
    )(ta, *fields)


def fold(recv):
    return pl.pallas_call(
        fold_kernel,
        out_shape=(shaped(4 * ROWS), shaped(3 * ROWS), shaped(3 * ROWS)),
        in_specs=[vmem()],
        out_specs=(vmem(), vmem(), vmem()),
        interpret=INTERPRET,
        name="fold",
    )(recv)


def compute(pos, stiff_table, perm_table, *blocks):
    cond_table = jnp.log2(perm_table) + (math.log2(0.5 * fine_dt) + SHARP * (1.0 - porosity_ref))
    return pl.pallas_call(
        main_kernel,
        out_shape=shaped(32 * 24),
        in_specs=[smem(), smem(), smem()] + [vmem()] * 5,
        out_specs=vmem(),
        scratch_shapes=[
            scratch(8 * SLOT + PAD),
            scratch(8 * SLOT + PAD),
            scratch(7 * SLOT + PAD),
            scratch(SLOT + PAD),
            scratch(SLOT + PAD),
            scratch(ROWS * PLANE),
            scratch(7 * FIELD + PAD),
            scratch(320),
        ],
        compiler_params=pltpu.CompilerParams(vmem_limit_bytes=58 << 20),
        interpret=INTERPRET,
        name="parareal",
    )(pos, stiff_table, cond_table, *blocks)


def unpack(recv):
    return pl.pallas_call(
        unpack_kernel,
        out_shape=shaped(320, 256),
        in_specs=[vmem()],
        out_specs=vmem(),
        scratch_shapes=[scratch(768)],
        interpret=INTERPRET,
        name="unpack",
    )(recv)


def shards(displacement, pressure, porosity, labels, ventricle_mask, stiff_table, perm_table):
    ta, gx, gy = (lax.axis_index(name).astype(jnp.int32) for name in ("ta", "gx", "gy"))
    flat = lambda a: a.reshape(a.shape[:-3] + (64, 256))
    sent = pack(
        ta.reshape(1), flat(displacement), flat(pressure), flat(porosity), flat(labels), flat(ventricle_mask)
    )
    got = lax.all_to_all(sent.reshape(4, ROWS, 128), "gy", 0, 0, tiled=True)
    own, down, up = fold(got.reshape(4 * ROWS, 128))

    def from_side(value, by):
        pairs = [(i, i - by) for i in range(8) if 0 <= i - by < 8]
        return lax.ppermute(value, "gx", pairs)

    blocks = (own, from_side(own, 1), from_side(own, -1), from_side(down, 2), from_side(up, -2))
    ends = compute(jnp.stack([gx * 8, ta * 32 + gy * 8]), stiff_table, perm_table, *blocks)
    mine = lax.all_to_all(ends.reshape(32, 24, 128), ("ta", "gy"), 0, 0, tiled=True)
    return unpack(mine.reshape(32 * 24, 128)).reshape(1, 5, 8, 8, 256)


def solution(mesh):
    placed = (
        P(None, "gx", "gy", None),
        P("gx", "gy", None),
        P("gx", "gy", None),
        P("gx", "gy", None),
        P("gx", "gy", None),
        P(),
        P(),
    )
    return jax.shard_map(
        shards,
        mesh=mesh,
        in_specs=placed,
        out_specs=P("ta", None, "gx", "gy", None),
        check_vma=False,
    )
```

```python
import math

import jax
import jax.numpy as jnp
from jax import lax
from jax.experimental import pallas as pl
from jax.experimental.pallas import tpu as pltpu
from jax.sharding import PartitionSpec as P

FINE = 4
coupling = 0.3
pressure_gain = 0.4
relax_rate = 0.5
stiffening = 2.0
porosity_ref = 0.2
fine_dt = 0.03

F32 = jnp.float32
INTERPRET = False

REACH = 18
ROWS = 128
PLANE = 24
FIELD = 19 * PLANE
SLOT = 6 * FIELD
PAD = 8 + 4 * PLANE
SHARP = stiffening * math.log2(math.e)
U_SCALE = fine_dt * relax_rate * 0.5
P_SCALE = U_SCALE * fine_dt * coupling * 0.5
GAIN = fine_dt * pressure_gain * relax_rate * 0.5 * P_SCALE / U_SCALE
MOVED = (0, 1, 2, 3, 5)


def lanes():
    return lax.broadcasted_iota(jnp.int32, (8, 128), 1)


def exchange_bits(v):
    lane = lanes()
    for b in range(2):
        high = ((lane >> (3 + b)) & 1) == 1
        step = 8 << b
        new = list(v)
        for i in range(4):
            if not (i >> b) & 1:
                j = i | (1 << b)
                new[i] = jnp.where(high, pltpu.roll(v[j], step, 1), v[i])
                new[j] = jnp.where(high, v[j], pltpu.roll(v[i], 128 - step, 1))
        v = new
    return v


def pack_kernel(ta_ref, disp, pres, poro, lab, mask, out, flat, big, win, rev):
    ta = ta_ref[0]
    zero = jnp.zeros((16, 128), F32)
    for f in range(7):
        field = disp[f] if f < 3 else (pres, poro, lab, mask)[f - 3][...].astype(F32)
        for h in range(2):
            flat[(f * 2 + h) * 64 : (f * 2 + h + 1) * 64, :] = field[:, h * 128 : (h + 1) * 128]

    def rows(f, h, xf):
        for xi in range(4):
            at = (f * 2 + h) * 64 + (4 + xi if xf else 3 - xi) * 8
            yield flat[at : at + 8, :]

    for t in range(4):
        one, two = 2 * t, min(2 * t + 1, 6)
        big[t * 288 : t * 288 + 16, :] = zero
        big[t * 288 + 272 : t * 288 + 288, :] = zero
        for h in range(2):
            parts = [part for xf in range(2) for f in (one, two) for part in rows(f, h, xf)]
            at = t * 288 + 16 + h * 128
            big[at : at + 128, :] = jnp.concatenate(parts, axis=0).T
        win[t * 64 : t * 64 + 64, :] = big[pl.ds(pl.multiple_of(t * 288 + ta * 32, 32), 64), :]
        for i in range(64):
            rev[t * 64 + i : t * 64 + i + 1, :] = win[t * 64 + 63 - i : t * 64 + 64 - i, :]
        win[256 + t * 64 : 320 + t * 64, :] = pltpu.roll(win[t * 64 : t * 64 + 64, :], 32, 1)
        rev[256 + t * 64 : 320 + t * 64, :] = pltpu.roll(rev[t * 64 : t * 64 + 64, :], 96, 1)
    near = (lax.broadcasted_iota(jnp.int32, (REACH, 128), 1) & 32) == 0
    for g in range(4):
        for f in range(7):
            t, odd = f // 2, f % 2
            low = 256 * odd + t * 64 + 44 - 8 * g
            high = 256 * (1 - odd) + t * 64 + 20 + 8 * g
            both = jnp.where(near, rev[low : low + REACH, :], win[high : high + REACH, :])
            out[g * ROWS + f * REACH : g * ROWS + (f + 1) * REACH, :] = both
        out[g * ROWS + 126 : g * ROWS + 128, :] = jnp.zeros((2, 128), F32)


def fold_kernel(recv, own, down, up):
    half0 = lanes() < 64

    def one(r):
        def at(i):
            return pl.ds(pl.multiple_of(i * ROWS + r * 8, 8), 8)

        v = exchange_bits([recv[at(gy), :] for gy in range(4)])
        for i in range(4):
            own[at(i), :] = v[i]
        for i in range(2):
            down[at(i), :] = v[i]
            up[at(i), :] = v[i]
        down[at(2), :] = jnp.where(half0, v[2], pltpu.roll(v[3], 64, 1))
        up[at(2), :] = jnp.where(half0, pltpu.roll(v[3], 64, 1), v[2])

    def group(r, carry):
        for i in range(4):
            one(r * 4 + i)
        return carry

    lax.fori_loop(0, ROWS // 32, group, 0)


def main_kernel(pos_ref, stiff_tab, cond_tab, own, east, west, east2, west2, out, a_st, b_st, c_st, t0, t1, raw, co):
    lane = lanes()
    row = lax.broadcasted_iota(jnp.int32, (8, 128), 0)
    half0 = lane < 64
    near_z = (lane & 32) == 0
    y = lane & 31
    has_n, has_s = y < 31, y > 0
    zero = jnp.zeros((8, 128), F32)

    def swap_x(v):
        return pltpu.roll(v, 64, 1)

    def swap_z(v):
        return jnp.where(near_z, pltpu.roll(v, 96, 1), pltpu.roll(v, 32, 1))

    def tile(start):
        return pl.ds(pl.multiple_of(start, 8), 8)

    def spread(r, carry):
        def get(ref, i):
            return ref[tile(i * ROWS + r * 8), :]

        def place(xi, v):
            raw[pl.ds(r * (8 * PLANE) + xi, 8, stride=PLANE), :] = v

        for i in range(4):
            place(i, get(own, i))
            place(4 + i, swap_x(jnp.where(half0, get(east, 3 - i), get(west, 3 - i))))
            place(8 + i, jnp.where(half0, get(west, i), get(east, i)))
        for i in range(2):
            place(14 + i, swap_x(jnp.where(half0, get(east2, 1 - i), get(west2, 1 - i))))
            place(16 + i, jnp.where(half0, get(west2, i), get(east2, i)))
        e, w = get(east2, 2), get(west2, 2)
        place(13, swap_x(jnp.where(half0, e, w)))
        place(12, jnp.where(half0, w, e))
        for i in range(6):
            place(18 + i, zero)
        return carry

    lax.fori_loop(0, ROWS // 8, spread, 0)

    x0, z0 = pos_ref[0], pos_ref[1]

    def coefficients(zi, carry):
        z = jnp.where(near_z, z0 + 3 - zi, z0 + 4 + zi)
        in_z = (z >= 0) & (z < 256)
        for b in range(3):
            xi = row + 8 * b
            x = jnp.where(half0, x0 + 3 - xi, x0 + 4 + xi)
            here = in_z & (x >= 0) & (x < 64)
            label = raw[tile((5 * REACH + zi) * PLANE + 8 * b), :]
            drain = raw[tile((6 * REACH + zi) * PLANE + 8 * b), :]
            stiff, cond = zero, zero
            for i in range(6):
                hit = label == float(i)
                stiff = jnp.where(hit, stiff_tab[i], stiff)
                cond = jnp.where(hit, cond_tab[i], cond)
            stiff = jnp.where(here, stiff, 0.0)
            fine_a = stiff * fine_dt
            coarse_a = stiff * (fine_dt * FINE)
            values = (
                fine_a,
                1.0 - 6.0 * fine_a,
                coarse_a,
                1.0 - 6.0 * coarse_a,
                jnp.where(here, 1.0 - drain, 0.0),
                jnp.where(here, cond, -1.0e30),
                jnp.where(here, 1.0, 0.0).astype(F32),
            )
            for i, value in enumerate(values):
                co[tile(i * FIELD + (zi + 1) * PLANE + 8 + 8 * b), :] = value
        return carry

    lax.fori_loop(0, REACH, coefficients, 0)

    sign_x = jnp.where(half0, -U_SCALE, U_SCALE).astype(F32)
    sign_z = jnp.where(near_z, -U_SCALE, U_SCALE).astype(F32)

    def where_of(slot, zi, b0=0):
        return pl.multiple_of(slot * SLOT + (zi + 1) * PLANE + 8 + 8 * b0, 8)

    def load(ref, at, f, off=0):
        return ref[pl.ds(at + (f * FIELD + off), 8), :]

    def coef(at, i, off):
        return co[pl.ds(at + (i * FIELD + off), 8), :]

    def put(ref, at, off, vals, k=None):
        for f in range(5):
            ref[pl.ds(at + (f * FIELD + off), 8), :] = vals[f]
        if k is not None:
            ref[pl.ds(at + (5 * FIELD + off), 8), :] = k

    def conduct(ca, off, psi):
        return jnp.exp2(coef(ca, 5, off) - psi)

    def begin(zi, carry):
        at, ca = where_of(0, zi), where_of(0, zi)
        for b in range(3):
            vals = [raw[tile((f * REACH + zi) * PLANE + 8 * b), :] for f in range(5)]
            vals[0] = vals[0] * sign_x
            vals[1] = vals[1] * U_SCALE
            vals[2] = vals[2] * sign_z
            vals[3] = vals[3] * P_SCALE
            vals[4] = (1.0 - vals[4]) * SHARP
            k = conduct(ca, 8 * b, vals[4])
            for ref in (a_st, t1):
                put(ref, at, 8 * b, vals, k)
        return carry

    lax.fori_loop(0, REACH, begin, 0)

    def north(v):
        return jnp.where(has_n, pltpu.roll(v, 127, 1), 0.0)

    def south(v):
        return jnp.where(has_s, pltpu.roll(v, 1, 1), 0.0)

    def advance(ref, slot, radius, fine, emit):
        units = (radius + 5) // 2
        passes = jnp.where(radius > 12, 2, 1)

        def unit(at, ca, carry):
            carry = list(carry)
            for d in range(2):
                for b in range(2):
                    off = d * PLANE + 8 * b
                    mid = {f: load(ref, at, f, off) for f in MOVED}
                    e = {f: load(ref, at, f, off + 1) for f in MOVED}
                    w = {f: load(ref, at, f, off - 1) for f in MOVED}
                    i = {f: load(ref, at, f, off + PLANE) for f in MOVED}
                    o = {f: load(ref, at, f, off - PLANE) for f in (0, 1, 2, 3)}
                    n, s = {}, {}
                    for j, f in enumerate(MOVED):
                        n[f] = north(mid[f])
                        s[f] = south(mid[f])
                    p, k = mid[3], mid[5]
                    face = (i[5] + k) * (i[3] - p)
                    flux = face - carry[b]
                    carry[b] = face
                    for side in (e, w, n, s):
                        flux = flux + (side[5] + k) * (side[3] - p)
                    dil = (e[0] - w[0]) + (n[1] - s[1]) + (i[2] - o[2])
                    m = coef(ca, 6, off)
                    grads = [e[3] - w[3], n[3] - s[3], i[3] - o[3]]
                    gain = GAIN
                    if not fine:
                        m = m * float(FINE)
                        grads[1] = grads[1] * float(FINE)
                        flux = flux * float(FINE)
                        gain = GAIN * FINE
                    grads[0] = grads[0] * m
                    grads[2] = grads[2] * m
                    a = coef(ca, 0 if fine else 2, off)
                    a6 = coef(ca, 1 if fine else 3, off)
                    new = []
                    for f in range(3):
                        around = (e[f] + w[f]) + (n[f] + s[f]) + (i[f] + o[f])
                        new.append(a * around + a6 * mid[f] - grads[f])
                    new.append(coef(ca, 4, off) * (p + (flux - gain * dil)))
                    psi = load(ref, at, 4, off)
                    new.append(psi * (1.0 - (dil if fine else dil * float(FINE))))
                    emit(at - slot * SLOT, ca, off, new)
            return tuple(carry)

        start = where_of(slot, 0)

        def ghost_x(f, zi):
            row0 = start + (f * FIELD + zi * PLANE)
            v = ref[pl.ds(row0, 8, stride=PLANE), :]
            ref[pl.ds(row0 - 1, 8, stride=PLANE), :] = swap_x(-v if f == 0 else v)

        def ghost_z(f, b):
            v = load(ref, start, f, 8 * b)
            v = swap_z(-v if f == 2 else v)
            ref[pl.ds(start + (f * FIELD + 8 * b - PLANE), 8), :] = v
            return v

        @pl.when(radius > 12)
        def _():
            for f in MOVED:
                ghost_z(f, 2)
                ghost_x(f, 10)

        def one_pass(j, c):
            b0 = passes - 1 - j
            at, ca = where_of(slot, 0, b0), where_of(0, 0, b0)
            for f in MOVED:
                ghost_x(f, 0)
                ghost_x(f, 8)
            for f in (0, 1, 2):
                for b in range(2):
                    ghost_z(f, b)
            carry = []
            for b in range(2):
                ghost_z(3, b)
                ghost_z(5, b)
            for b in range(2):
                k0, k1 = load(ref, at, 5, 8 * b - PLANE), load(ref, at, 5, 8 * b)
                p0, p1 = load(ref, at, 3, 8 * b - PLANE), load(ref, at, 3, 8 * b)
                carry.append((k0 + k1) * (p1 - p0))

            def step(u, carry):
                shift = u * (2 * PLANE)
                return unit(pl.multiple_of(at + shift, 8), pl.multiple_of(ca + shift, 8), carry)

            lax.fori_loop(0, units, step, tuple(carry))
            return c

        lax.fori_loop(0, passes, one_pass, 0)

    def slot_at(slot, at):
        return pl.multiple_of(slot * SLOT + at, 8)

    def plain(src, slot, radius, fine, *targets):
        def emit(at, ca, off, new):
            k = conduct(ca, off, new[4])
            for ref, to in targets:
                put(ref, slot_at(to, at), off, new, k)

        advance(src, slot, radius, fine, emit)

    def minus(src, slot, radius, sub, to):
        def emit(at, ca, off, new):
            old = slot_at(sub, at)
            put(c_st, slot_at(to, at), off, [new[f] - load(a_st, old, f, off) for f in range(5)])

        advance(src, slot, radius, True, emit)

    def plus(src, radius, cor, keep, *targets):
        def emit(at, ca, off, new):
            if keep is not None:
                put(a_st, slot_at(keep, at), off, new)
            if targets:
                old = slot_at(cor, at)
                vals = [new[f] + load(c_st, old, f, off) for f in range(5)]
                k = conduct(ca, off, vals[4])
                for ref, to in targets:
                    put(ref, slot_at(to, at), off, vals, k)

        advance(src, 0, radius, False, emit)

    def fine_all(source, base, start):
        def slab(j, carry):
            plain(source, base + j, start - j, True, (t0, 0))
            plain(t0, 0, start - 1 - j, True, (t1, 0))
            plain(t1, 0, start - 2 - j, True, (t0, 0))
            minus(t0, 0, start - 3 - j, j + 1, j)

            @pl.when(j == 0)
            def _():
                for zi in range(4):
                    put(b_st, where_of(0, zi), 0, [load(b_st, where_of(1, zi), f) for f in range(5)])

                def body(zi, carry):
                    at = where_of(0, zi)
                    for b in range(2):
                        off = 8 * b
                        vals = [load(a_st, slot_at(1, at), f, off) + load(c_st, at, f, off) for f in range(5)]
                        put(b_st, slot_at(1, at), off, vals, conduct(at, off, vals[4]))
                    return carry

                lax.fori_loop(0, start + 1, body, 0)

            return carry

        lax.fori_loop(0, 7, slab, 0)

    def restart():
        def step(i, carry):
            for j in range(9):
                at = i * 72 + 8 * j
                t1[tile(at), :] = b_st[tile(SLOT + at), :]
            return carry

        lax.fori_loop(0, SLOT // 72, step, 0)

    def chain0(i, carry):
        k = 2 * i
        plain(t1, 0, 13 - k, False, (t0, 0), (a_st, k + 1))
        plain(t0, 0, 12 - k, False, (t1, 0), (a_st, k + 2))
        return carry

    lax.fori_loop(0, 3, chain0, 0)
    plain(t1, 0, jnp.int32(4), False, (a_st, 7))
    fine_all(a_st, 0, 13)
    restart()

    def chain1(i, carry):
        k = 2 * i + 1
        plus(t1, 10 - k, k, k, (t0, 0), (b_st, k + 1))
        plus(t0, 9 - k, k + 1, k + 1, (t1, 0), (b_st, k + 2))
        return carry

    lax.fori_loop(0, 3, chain1, 0)
    plus(t1, jnp.int32(0), None, 7)
    fine_all(b_st, 1, 9)
    restart()

    def chain2(i, carry):
        k = 2 * i + 2
        plus(t1, 7 - k, k - 1, None, (t0, 0), (b_st, k))
        plus(t0, 6 - k, k, None, (t1, 0), (b_st, k + 1))
        return carry

    lax.fori_loop(0, 3, chain2, 0)

    unsign_x = jnp.where(half0, -1.0 / U_SCALE, 1.0 / U_SCALE).astype(F32)
    unsign_z = jnp.where(near_z, -1.0 / U_SCALE, 1.0 / U_SCALE).astype(F32)
    for f in range(5):
        for zi in range(4):
            v = []
            for xi in range(4):
                e = b_st[pl.ds(f * FIELD + (zi + 1) * PLANE + 8 + xi, 8, stride=SLOT), :]
                if f == 4:
                    e = 1.0 - e * (1.0 / SHARP)
                else:
                    e = e * (unsign_x, 1.0 / U_SCALE, unsign_z, 1.0 / P_SCALE)[f]
                v.append(e)
            v = exchange_bits(v)
            for gy in range(4):
                out[pl.ds(gy * 24 + f * 4 + zi, 8, stride=96), :] = v[gy]
    for i in range(32):
        out[i * 24 + 20 : i * 24 + 24, :] = jnp.zeros((4, 128), F32)


def unpack_kernel(recv, out, rows):
    near_z = (lanes() & 32) == 0
    for t in range(3):
        for zi in range(4):
            for g in range(4):
                one = recv[pl.ds(g * 192 + 2 * t * 4 + zi, 8, stride=24), :]
                two = recv[pl.ds(g * 192 + min(2 * t + 1, 4) * 4 + zi, 8, stride=24), :]
                low = jnp.where(near_z, one, pltpu.roll(two, 32, 1))
                high = jnp.where(near_z, pltpu.roll(one, 96, 1), two)
                rows[pl.ds(t * 256 + g * 64 + 3 - zi, 8, stride=8), :] = low
                rows[pl.ds(t * 256 + g * 64 + 4 + zi, 8, stride=8), :] = high
        for h in range(2):
            block = rows[t * 256 + h * 128 : t * 256 + (h + 1) * 128, :].T
            for i in range(1 if t == 2 else 2):
                for xf in range(2):
                    for xi in range(4):
                        at = ((2 * t + i) * 8 + (4 + xi if xf else 3 - xi)) * 8
                        source = xf * 64 + i * 32 + xi * 8
                        out[at : at + 8, h * 128 : (h + 1) * 128] = block[source : source + 8, :]


def vmem():
    return pl.BlockSpec(memory_space=pltpu.VMEM)


def smem():
    return pl.BlockSpec(memory_space=pltpu.SMEM)


def scratch(rows):
    return pltpu.VMEM((rows, 128), F32)


def shaped(rows, width=128):
    return jax.ShapeDtypeStruct((rows, width), F32)


def pack(ta, *fields):
    return pl.pallas_call(
        pack_kernel,
        out_shape=shaped(4 * ROWS),
        in_specs=[smem()] + [vmem()] * 5,
        out_specs=vmem(),
        scratch_shapes=[scratch(896), scratch(1152), scratch(512), scratch(512)],
        compiler_params=pltpu.CompilerParams(vmem_limit_bytes=8 << 20),
        interpret=INTERPRET,
        name="pack",
    )(ta, *fields)


def fold(recv):
    return pl.pallas_call(
        fold_kernel,
        out_shape=(shaped(4 * ROWS), shaped(3 * ROWS), shaped(3 * ROWS)),
        in_specs=[vmem()],
        out_specs=(vmem(), vmem(), vmem()),
        compiler_params=pltpu.CompilerParams(vmem_limit_bytes=8 << 20),
        interpret=INTERPRET,
        name="fold",
    )(recv)


def compute(pos, stiff_table, perm_table, *blocks):
    cond_table = jnp.log2(perm_table) + (math.log2(0.5 * fine_dt) + SHARP * (1.0 - porosity_ref))
    return pl.pallas_call(
        main_kernel,
        out_shape=shaped(32 * 24),
        in_specs=[smem(), smem(), smem()] + [vmem()] * 5,
        out_specs=vmem(),
        scratch_shapes=[
            scratch(8 * SLOT + PAD),
            scratch(8 * SLOT + PAD),
            scratch(7 * SLOT + PAD),
            scratch(SLOT + PAD),
            scratch(SLOT + PAD),
            scratch(ROWS * PLANE),
            scratch(7 * FIELD + PAD),
        ],
        compiler_params=pltpu.CompilerParams(vmem_limit_bytes=42 << 20),
        interpret=INTERPRET,
        name="parareal",
    )(pos, stiff_table, cond_table, *blocks)


def unpack(recv):
    return pl.pallas_call(
        unpack_kernel,
        out_shape=shaped(320, 256),
        in_specs=[vmem()],
        out_specs=vmem(),
        scratch_shapes=[scratch(768)],
        compiler_params=pltpu.CompilerParams(vmem_limit_bytes=8 << 20),
        interpret=INTERPRET,
        name="unpack",
    )(recv)


def shards(displacement, pressure, porosity, labels, ventricle_mask, stiff_table, perm_table):
    ta, gx, gy = (lax.axis_index(name).astype(jnp.int32) for name in ("ta", "gx", "gy"))
    flat = lambda a: a.reshape(a.shape[:-3] + (64, 256))
    sent = pack(
        ta.reshape(1), flat(displacement), flat(pressure), flat(porosity), flat(labels), flat(ventricle_mask)
    )
    got = lax.all_to_all(sent.reshape(4, ROWS, 128), "gy", 0, 0, tiled=True)
    own, down, up = fold(got.reshape(4 * ROWS, 128))

    def from_side(value, by):
        pairs = [(i, i - by) for i in range(8) if 0 <= i - by < 8]
        return lax.ppermute(value, "gx", pairs)

    blocks = (own, from_side(own, 1), from_side(own, -1), from_side(down, 2), from_side(up, -2))
    ends = compute(jnp.stack([gx * 8, ta * 32 + gy * 8]), stiff_table, perm_table, *blocks)
    mine = lax.all_to_all(ends.reshape(32, 24, 128), ("ta", "gy"), 0, 0, tiled=True)
    return unpack(mine.reshape(32 * 24, 128)).reshape(1, 5, 8, 8, 256)


def solution(mesh):
    placed = (
        P(None, "gx", "gy", None),
        P("gx", "gy", None),
        P("gx", "gy", None),
        P("gx", "gy", None),
        P("gx", "gy", None),
        P(),
        P(),
    )
    return jax.shard_map(
        shards,
        mesh=mesh,
        in_specs=placed,
        out_specs=P("ta", None, "gx", "gy", None),
        check_vma=False,
    )
```

```python
import math

import jax
import jax.numpy as jnp
from jax import lax
from jax.experimental import pallas as pl
from jax.experimental.pallas import tpu as pltpu
from jax.sharding import PartitionSpec as P

FINE = 4
coupling = 0.3
pressure_gain = 0.4
relax_rate = 0.5
stiffening = 2.0
porosity_ref = 0.2
fine_dt = 0.03

F32 = jnp.float32
INTERPRET = False

REACH = 18
ROWS = 128
PLANE = 24
FIELD = 19 * PLANE
SLOT = 6 * FIELD
PAD = 8 + 4 * PLANE
SHARP = stiffening * math.log2(math.e)
U_SCALE = fine_dt * relax_rate * 0.5
P_SCALE = U_SCALE * fine_dt * coupling * 0.5
GAIN = fine_dt * pressure_gain * relax_rate * 0.5 * P_SCALE / U_SCALE
MOVED = (0, 1, 2, 3, 5)


def lanes():
    return lax.broadcasted_iota(jnp.int32, (8, 128), 1)


def exchange_bits(v):
    lane = lanes()
    for b in range(2):
        high = ((lane >> (3 + b)) & 1) == 1
        step = 8 << b
        new = list(v)
        for i in range(4):
            if not (i >> b) & 1:
                j = i | (1 << b)
                new[i] = jnp.where(high, pltpu.roll(v[j], step, 1), v[i])
                new[j] = jnp.where(high, v[j], pltpu.roll(v[i], 128 - step, 1))
        v = new
    return v


def pack_kernel(ta_ref, disp, pres, poro, lab, mask, out, flat, big, win, rev):
    ta = ta_ref[0]
    zero = jnp.zeros((16, 128), F32)
    for f in range(7):
        field = disp[f] if f < 3 else (pres, poro, lab, mask)[f - 3][...].astype(F32)
        for h in range(2):
            flat[(f * 2 + h) * 64 : (f * 2 + h + 1) * 64, :] = field[:, h * 128 : (h + 1) * 128]

    def rows(f, h, xf):
        for xi in range(4):
            at = (f * 2 + h) * 64 + (4 + xi if xf else 3 - xi) * 8
            yield flat[at : at + 8, :]

    for t in range(4):
        one, two = 2 * t, min(2 * t + 1, 6)
        big[t * 288 : t * 288 + 16, :] = zero
        big[t * 288 + 272 : t * 288 + 288, :] = zero
        for h in range(2):
            parts = [part for xf in range(2) for f in (one, two) for part in rows(f, h, xf)]
            at = t * 288 + 16 + h * 128
            big[at : at + 128, :] = jnp.concatenate(parts, axis=0).T
        win[t * 64 : t * 64 + 64, :] = big[pl.ds(pl.multiple_of(t * 288 + ta * 32, 32), 64), :]
        for i in range(64):
            rev[t * 64 + i : t * 64 + i + 1, :] = win[t * 64 + 63 - i : t * 64 + 64 - i, :]
        win[256 + t * 64 : 320 + t * 64, :] = pltpu.roll(win[t * 64 : t * 64 + 64, :], 32, 1)
        rev[256 + t * 64 : 320 + t * 64, :] = pltpu.roll(rev[t * 64 : t * 64 + 64, :], 96, 1)
    near = (lax.broadcasted_iota(jnp.int32, (REACH, 128), 1) & 32) == 0
    for g in range(4):
        for f in range(7):
            t, odd = f // 2, f % 2
            low = 256 * odd + t * 64 + 44 - 8 * g
            high = 256 * (1 - odd) + t * 64 + 20 + 8 * g
            both = jnp.where(near, rev[low : low + REACH, :], win[high : high + REACH, :])
            out[g * ROWS + f * REACH : g * ROWS + (f + 1) * REACH, :] = both
        out[g * ROWS + 126 : g * ROWS + 128, :] = jnp.zeros((2, 128), F32)


def fold_kernel(recv, own, down, up):
    half0 = lanes() < 64

    def one(r):
        def at(i):
            return pl.ds(pl.multiple_of(i * ROWS + r * 8, 8), 8)

        v = exchange_bits([recv[at(gy), :] for gy in range(4)])
        for i in range(4):
            own[at(i), :] = v[i]
        for i in range(2):
            down[at(i), :] = v[i]
            up[at(i), :] = v[i]
        down[at(2), :] = jnp.where(half0, v[2], pltpu.roll(v[3], 64, 1))
        up[at(2), :] = jnp.where(half0, pltpu.roll(v[3], 64, 1), v[2])

    def group(r, carry):
        for i in range(4):
            one(r * 4 + i)
        return carry

    lax.fori_loop(0, ROWS // 32, group, 0)


def main_kernel(pos_ref, stiff_tab, cond_tab, own, east, west, east2, west2, out, a_st, b_st, c_st, t0, t1, raw, co):
    lane = lanes()
    row = lax.broadcasted_iota(jnp.int32, (8, 128), 0)
    half0 = lane < 64
    near_z = (lane & 32) == 0
    y = lane & 31
    has_n, has_s = y < 31, y > 0
    zero = jnp.zeros((8, 128), F32)

    def swap_x(v):
        return pltpu.roll(v, 64, 1)

    def swap_z(v):
        return jnp.where(near_z, pltpu.roll(v, 96, 1), pltpu.roll(v, 32, 1))

    def tile(start):
        return pl.ds(pl.multiple_of(start, 8), 8)

    def spread(r, carry):
        def get(ref, i):
            return ref[tile(i * ROWS + r * 8), :]

        def place(xi, v):
            raw[pl.ds(r * (8 * PLANE) + xi, 8, stride=PLANE), :] = v

        for i in range(4):
            place(i, get(own, i))
            place(4 + i, swap_x(jnp.where(half0, get(east, 3 - i), get(west, 3 - i))))
            place(8 + i, jnp.where(half0, get(west, i), get(east, i)))
        for i in range(2):
            place(14 + i, swap_x(jnp.where(half0, get(east2, 1 - i), get(west2, 1 - i))))
            place(16 + i, jnp.where(half0, get(west2, i), get(east2, i)))
        e, w = get(east2, 2), get(west2, 2)
        place(13, swap_x(jnp.where(half0, e, w)))
        place(12, jnp.where(half0, w, e))
        for i in range(6):
            place(18 + i, zero)
        return carry

    lax.fori_loop(0, ROWS // 8, spread, 0)

    x0, z0 = pos_ref[0], pos_ref[1]

    def coefficients(zi, carry):
        z = jnp.where(near_z, z0 + 3 - zi, z0 + 4 + zi)
        in_z = (z >= 0) & (z < 256)
        for b in range(3):
            xi = row + 8 * b
            x = jnp.where(half0, x0 + 3 - xi, x0 + 4 + xi)
            here = in_z & (x >= 0) & (x < 64)
            label = raw[tile((5 * REACH + zi) * PLANE + 8 * b), :]
            drain = raw[tile((6 * REACH + zi) * PLANE + 8 * b), :]
            stiff, cond = zero, zero
            for i in range(6):
                hit = label == float(i)
                stiff = jnp.where(hit, stiff_tab[i], stiff)
                cond = jnp.where(hit, cond_tab[i], cond)
            stiff = jnp.where(here, stiff, 0.0)
            fine_a = stiff * fine_dt
            coarse_a = stiff * (fine_dt * FINE)
            values = (
                fine_a,
                1.0 - 6.0 * fine_a,
                coarse_a,
                1.0 - 6.0 * coarse_a,
                jnp.where(here, 1.0 - drain, 0.0),
                jnp.where(here, cond, -1.0e30),
                jnp.where(here, 1.0, 0.0).astype(F32),
            )
            for i, value in enumerate(values):
                co[tile(i * FIELD + (zi + 1) * PLANE + 8 + 8 * b), :] = value
        return carry

    lax.fori_loop(0, REACH, coefficients, 0)

    sign_x = jnp.where(half0, -U_SCALE, U_SCALE).astype(F32)
    sign_z = jnp.where(near_z, -U_SCALE, U_SCALE).astype(F32)

    def where_of(slot, zi, b0=0):
        return pl.multiple_of(slot * SLOT + (zi + 1) * PLANE + 8 + 8 * b0, 8)

    def load(ref, at, f, off=0):
        return ref[pl.ds(at + (f * FIELD + off), 8), :]

    def coef(at, i, off):
        return co[pl.ds(at + (i * FIELD + off), 8), :]

    def put(ref, at, off, vals, k=None):
        for f in range(5):
            ref[pl.ds(at + (f * FIELD + off), 8), :] = vals[f]
        if k is not None:
            ref[pl.ds(at + (5 * FIELD + off), 8), :] = k

    def conduct(ca, off, psi):
        return jnp.exp2(coef(ca, 5, off) - psi)

    def begin(zi, carry):
        at, ca = where_of(0, zi), where_of(0, zi)
        for b in range(3):
            vals = [raw[tile((f * REACH + zi) * PLANE + 8 * b), :] for f in range(5)]
            vals[0] = vals[0] * sign_x
            vals[1] = vals[1] * U_SCALE
            vals[2] = vals[2] * sign_z
            vals[3] = vals[3] * P_SCALE
            vals[4] = (1.0 - vals[4]) * SHARP
            k = conduct(ca, 8 * b, vals[4])
            for ref in (a_st, t1):
                put(ref, at, 8 * b, vals, k)
        return carry

    lax.fori_loop(0, REACH, begin, 0)

    def north(v):
        return jnp.where(has_n, pltpu.roll(v, 127, 1), 0.0)

    def south(v):
        return jnp.where(has_s, pltpu.roll(v, 1, 1), 0.0)

    def advance(ref, slot, radius, fine, emit):
        units = (radius + 5) // 2
        passes = jnp.where(radius > 12, 2, 1)

        def unit(at, ca, carry):
            carry = list(carry)
            for d in range(2):
                for b in range(2):
                    off = d * PLANE + 8 * b
                    mid = {f: load(ref, at, f, off) for f in MOVED}
                    e = {f: load(ref, at, f, off + 1) for f in MOVED}
                    w = {f: load(ref, at, f, off - 1) for f in MOVED}
                    i = {f: load(ref, at, f, off + PLANE) for f in MOVED}
                    o = {f: load(ref, at, f, off - PLANE) for f in (0, 1, 2, 3)}
                    n, s = {}, {}
                    for j, f in enumerate(MOVED):
                        n[f] = north(mid[f])
                        s[f] = south(mid[f])
                    p, k = mid[3], mid[5]
                    face = (i[5] + k) * (i[3] - p)
                    flux = face - carry[b]
                    carry[b] = face
                    for side in (e, w, n, s):
                        flux = flux + (side[5] + k) * (side[3] - p)
                    dil = (e[0] - w[0]) + (n[1] - s[1]) + (i[2] - o[2])
                    m = coef(ca, 6, off)
                    grads = [e[3] - w[3], n[3] - s[3], i[3] - o[3]]
                    gain = GAIN
                    if not fine:
                        m = m * float(FINE)
                        grads[1] = grads[1] * float(FINE)
                        flux = flux * float(FINE)
                        gain = GAIN * FINE
                    grads[0] = grads[0] * m
                    grads[2] = grads[2] * m
                    a = coef(ca, 0 if fine else 2, off)
                    a6 = coef(ca, 1 if fine else 3, off)
                    new = []
                    for f in range(3):
                        around = (e[f] + w[f]) + (n[f] + s[f]) + (i[f] + o[f])
                        new.append(a * around + a6 * mid[f] - grads[f])
                    new.append(coef(ca, 4, off) * (p + (flux - gain * dil)))
                    psi = load(ref, at, 4, off)
                    new.append(psi * (1.0 - (dil if fine else dil * float(FINE))))
                    emit(at - slot * SLOT, ca, off, new)
            return tuple(carry)

        start = where_of(slot, 0)

        def ghost_x(f, zi):
            row0 = start + (f * FIELD + zi * PLANE)
            v = ref[pl.ds(row0, 8, stride=PLANE), :]
            ref[pl.ds(row0 - 1, 8, stride=PLANE), :] = swap_x(-v if f == 0 else v)

        def ghost_z(f, b):
            v = load(ref, start, f, 8 * b)
            v = swap_z(-v if f == 2 else v)
            ref[pl.ds(start + (f * FIELD + 8 * b - PLANE), 8), :] = v
            return v

        @pl.when(radius > 12)
        def _():
            for f in MOVED:
                ghost_z(f, 2)
                ghost_x(f, 10)

        def one_pass(j, c):
            b0 = passes - 1 - j
            at, ca = where_of(slot, 0, b0), where_of(0, 0, b0)
            for f in MOVED:
                ghost_x(f, 0)
                ghost_x(f, 8)
            for f in (0, 1, 2):
                for b in range(2):
                    ghost_z(f, b)
            carry = []
            for b in range(2):
                ghost_z(3, b)
                ghost_z(5, b)
            for b in range(2):
                k0, k1 = load(ref, at, 5, 8 * b - PLANE), load(ref, at, 5, 8 * b)
                p0, p1 = load(ref, at, 3, 8 * b - PLANE), load(ref, at, 3, 8 * b)
                carry.append((k0 + k1) * (p1 - p0))

            def moved(u, carry):
                shift = u * (2 * PLANE)
                return unit(pl.multiple_of(at + shift, 8), pl.multiple_of(ca + shift, 8), carry)

            def two(u, carry):
                return moved(2 * u + 1, moved(2 * u, carry))

            carry = lax.fori_loop(0, units // 2, two, tuple(carry))

            @pl.when(units % 2 == 1)
            def _():
                moved(units - 1, carry)

            return c

        lax.fori_loop(0, passes, one_pass, 0)

    def slot_at(slot, at):
        return pl.multiple_of(slot * SLOT + at, 8)

    def plain(src, slot, radius, fine, *targets):
        def emit(at, ca, off, new):
            k = conduct(ca, off, new[4])
            for ref, to in targets:
                put(ref, slot_at(to, at), off, new, k)

        advance(src, slot, radius, fine, emit)

    def minus(src, slot, radius, sub, to):
        def emit(at, ca, off, new):
            old = slot_at(sub, at)
            put(c_st, slot_at(to, at), off, [new[f] - load(a_st, old, f, off) for f in range(5)])

        advance(src, slot, radius, True, emit)

    def plus(src, radius, cor, keep, *targets):
        def emit(at, ca, off, new):
            if keep is not None:
                put(a_st, slot_at(keep, at), off, new)
            if targets:
                old = slot_at(cor, at)
                vals = [new[f] + load(c_st, old, f, off) for f in range(5)]
                k = conduct(ca, off, vals[4])
                for ref, to in targets:
                    put(ref, slot_at(to, at), off, vals, k)

        advance(src, 0, radius, False, emit)

    def fine_all(source, base, start):
        def slab(j, carry):
            plain(source, base + j, start - j, True, (t0, 0))
            plain(t0, 0, start - 1 - j, True, (t1, 0))
            plain(t1, 0, start - 2 - j, True, (t0, 0))
            minus(t0, 0, start - 3 - j, j + 1, j)

            @pl.when(j == 0)
            def _():
                for zi in range(4):
                    put(b_st, where_of(0, zi), 0, [load(b_st, where_of(1, zi), f) for f in range(5)])

                def body(zi, carry):
                    at = where_of(0, zi)
                    for b in range(2):
                        off = 8 * b
                        vals = [load(a_st, slot_at(1, at), f, off) + load(c_st, at, f, off) for f in range(5)]
                        put(b_st, slot_at(1, at), off, vals, conduct(at, off, vals[4]))
                    return carry

                lax.fori_loop(0, start + 1, body, 0)

            return carry

        lax.fori_loop(0, 7, slab, 0)

    def restart():
        def step(i, carry):
            for j in range(9):
                at = i * 72 + 8 * j
                t1[tile(at), :] = b_st[tile(SLOT + at), :]
            return carry

        lax.fori_loop(0, SLOT // 72, step, 0)

    def chain0(i, carry):
        k = 2 * i
        plain(t1, 0, 13 - k, False, (t0, 0), (a_st, k + 1))
        plain(t0, 0, 12 - k, False, (t1, 0), (a_st, k + 2))
        return carry

    lax.fori_loop(0, 3, chain0, 0)
    plain(t1, 0, jnp.int32(4), False, (a_st, 7))
    fine_all(a_st, 0, 13)
    restart()

    def chain1(i, carry):
        k = 2 * i + 1
        plus(t1, 10 - k, k, k, (t0, 0), (b_st, k + 1))
        plus(t0, 9 - k, k + 1, k + 1, (t1, 0), (b_st, k + 2))
        return carry

    lax.fori_loop(0, 3, chain1, 0)
    plus(t1, jnp.int32(0), None, 7)
    fine_all(b_st, 1, 9)
    restart()

    def chain2(i, carry):
        k = 2 * i + 2
        plus(t1, 7 - k, k - 1, None, (t0, 0), (b_st, k))
        plus(t0, 6 - k, k, None, (t1, 0), (b_st, k + 1))
        return carry

    lax.fori_loop(0, 3, chain2, 0)

    unsign_x = jnp.where(half0, -1.0 / U_SCALE, 1.0 / U_SCALE).astype(F32)
    unsign_z = jnp.where(near_z, -1.0 / U_SCALE, 1.0 / U_SCALE).astype(F32)
    for f in range(5):
        for zi in range(4):
            v = []
            for xi in range(4):
                e = b_st[pl.ds(f * FIELD + (zi + 1) * PLANE + 8 + xi, 8, stride=SLOT), :]
                if f == 4:
                    e = 1.0 - e * (1.0 / SHARP)
                else:
                    e = e * (unsign_x, 1.0 / U_SCALE, unsign_z, 1.0 / P_SCALE)[f]
                v.append(e)
            v = exchange_bits(v)
            for gy in range(4):
                out[pl.ds(gy * 20 + f * 4 + zi, 8, stride=80), :] = v[gy]


def unpack_kernel(recv, out, rows):
    near_z = (lanes() & 32) == 0
    for t in range(3):
        for zi in range(4):
            for g in range(4):
                one = recv[pl.ds(g * 160 + 2 * t * 4 + zi, 8, stride=20), :]
                two = recv[pl.ds(g * 160 + min(2 * t + 1, 4) * 4 + zi, 8, stride=20), :]
                low = jnp.where(near_z, one, pltpu.roll(two, 32, 1))
                high = jnp.where(near_z, pltpu.roll(one, 96, 1), two)
                rows[pl.ds(t * 256 + g * 64 + 3 - zi, 8, stride=8), :] = low
                rows[pl.ds(t * 256 + g * 64 + 4 + zi, 8, stride=8), :] = high
        for h in range(2):
            block = rows[t * 256 + h * 128 : t * 256 + (h + 1) * 128, :].T
            for i in range(1 if t == 2 else 2):
                for xf in range(2):
                    for xi in range(4):
                        at = ((2 * t + i) * 8 + (4 + xi if xf else 3 - xi)) * 8
                        source = xf * 64 + i * 32 + xi * 8
                        out[at : at + 8, h * 128 : (h + 1) * 128] = block[source : source + 8, :]


def vmem():
    return pl.BlockSpec(memory_space=pltpu.VMEM)


def smem():
    return pl.BlockSpec(memory_space=pltpu.SMEM)


def scratch(rows):
    return pltpu.VMEM((rows, 128), F32)


def shaped(rows, width=128):
    return jax.ShapeDtypeStruct((rows, width), F32)


def pack(ta, *fields):
    return pl.pallas_call(
        pack_kernel,
        out_shape=shaped(4 * ROWS),
        in_specs=[smem()] + [vmem()] * 5,
        out_specs=vmem(),
        scratch_shapes=[scratch(896), scratch(1152), scratch(512), scratch(512)],
        interpret=INTERPRET,
        name="pack",
    )(ta, *fields)


def fold(recv):
    return pl.pallas_call(
        fold_kernel,
        out_shape=(shaped(4 * ROWS), shaped(3 * ROWS), shaped(3 * ROWS)),
        in_specs=[vmem()],
        out_specs=(vmem(), vmem(), vmem()),
        compiler_params=pltpu.CompilerParams(vmem_limit_bytes=8 << 20),
        interpret=INTERPRET,
        name="fold",
    )(recv)


def compute(pos, stiff_table, perm_table, *blocks):
    cond_table = jnp.log2(perm_table) + (math.log2(0.5 * fine_dt) + SHARP * (1.0 - porosity_ref))
    return pl.pallas_call(
        main_kernel,
        out_shape=shaped(32 * 20),
        in_specs=[smem(), smem(), smem()] + [vmem()] * 5,
        out_specs=vmem(),
        scratch_shapes=[
            scratch(8 * SLOT + PAD),
            scratch(8 * SLOT + PAD),
            scratch(7 * SLOT + PAD),
            scratch(SLOT + PAD),
            scratch(SLOT + PAD),
            scratch(ROWS * PLANE),
            scratch(7 * FIELD + PAD),
        ],
        compiler_params=pltpu.CompilerParams(vmem_limit_bytes=42 << 20),
        interpret=INTERPRET,
        name="parareal",
    )(pos, stiff_table, cond_table, *blocks)


def unpack(recv):
    return pl.pallas_call(
        unpack_kernel,
        out_shape=shaped(320, 256),
        in_specs=[vmem()],
        out_specs=vmem(),
        scratch_shapes=[scratch(768)],
        compiler_params=pltpu.CompilerParams(vmem_limit_bytes=8 << 20),
        interpret=INTERPRET,
        name="unpack",
    )(recv)


def shards(displacement, pressure, porosity, labels, ventricle_mask, stiff_table, perm_table):
    ta, gx, gy = (lax.axis_index(name).astype(jnp.int32) for name in ("ta", "gx", "gy"))
    flat = lambda a: a.reshape(a.shape[:-3] + (64, 256))
    sent = pack(
        ta.reshape(1), flat(displacement), flat(pressure), flat(porosity), flat(labels), flat(ventricle_mask)
    )
    got = lax.all_to_all(sent.reshape(4, ROWS, 128), "gy", 0, 0, tiled=True)
    own, down, up = fold(got.reshape(4 * ROWS, 128))

    def from_side(value, by):
        pairs = [(i, i - by) for i in range(8) if 0 <= i - by < 8]
        return lax.ppermute(value, "gx", pairs)

    blocks = (own, from_side(own, 1), from_side(own, -1), from_side(down, 2), from_side(up, -2))
    ends = compute(jnp.stack([gx * 8, ta * 32 + gy * 8]), stiff_table, perm_table, *blocks)
    mine = lax.all_to_all(ends.reshape(32, 5, 4, 128), ("ta", "gy"), 0, 0, tiled=True)
    return unpack(mine.reshape(32 * 20, 128)).reshape(1, 5, 8, 8, 256)


def solution(mesh):
    placed = (
        P(None, "gx", "gy", None),
        P("gx", "gy", None),
        P("gx", "gy", None),
        P("gx", "gy", None),
        P("gx", "gy", None),
        P(),
        P(),
    )
    return jax.shard_map(
        shards,
        mesh=mesh,
        in_specs=placed,
        out_specs=P("ta", None, "gx", "gy", None),
        check_vma=False,
    )
```

```python
import math

import jax
import jax.numpy as jnp
from jax import lax
from jax.experimental import pallas as pl
from jax.experimental.pallas import tpu as pltpu
from jax.sharding import PartitionSpec as P

FINE = 4
coupling = 0.3
pressure_gain = 0.4
relax_rate = 0.5
stiffening = 2.0
porosity_ref = 0.2
fine_dt = 0.03

F32 = jnp.float32
INTERPRET = False

REACH = 18
ROWS = 128
FAR = 64
PLANE = 24
FIELD = 19 * PLANE
SLOT = 6 * FIELD
PAD = 8 + 4 * PLANE
SHARP = stiffening * math.log2(math.e)
U_SCALE = fine_dt * relax_rate * 0.5
P_SCALE = U_SCALE * fine_dt * coupling * 0.5
GAIN = fine_dt * pressure_gain * relax_rate * 0.5 * P_SCALE / U_SCALE
MOVED = (0, 1, 2, 3, 5)


def lanes():
    return lax.broadcasted_iota(jnp.int32, (8, 128), 1)


def exchange_bits(v):
    lane = lanes()
    for b in range(2):
        high = ((lane >> (3 + b)) & 1) == 1
        step = 8 << b
        new = list(v)
        for i in range(4):
            if not (i >> b) & 1:
                j = i | (1 << b)
                new[i] = jnp.where(high, pltpu.roll(v[j], step, 1), v[i])
                new[j] = jnp.where(high, v[j], pltpu.roll(v[i], 128 - step, 1))
        v = new
    return v


def pack_kernel(ta_ref, disp, pres, poro, lab, mask, out, flat, big, win, rev):
    ta = ta_ref[0]
    zero = jnp.zeros((16, 128), F32)
    for f in range(7):
        field = disp[f] if f < 3 else (pres, poro, lab, mask)[f - 3][...].astype(F32)
        for h in range(2):
            flat[(f * 2 + h) * 64 : (f * 2 + h + 1) * 64, :] = field[:, h * 128 : (h + 1) * 128]

    def rows(f, h, xf):
        for xi in range(4):
            at = (f * 2 + h) * 64 + (4 + xi if xf else 3 - xi) * 8
            yield flat[at : at + 8, :]

    for t in range(4):
        one, two = 2 * t, min(2 * t + 1, 6)
        big[t * 288 : t * 288 + 16, :] = zero
        big[t * 288 + 272 : t * 288 + 288, :] = zero
        for h in range(2):
            parts = [part for xf in range(2) for f in (one, two) for part in rows(f, h, xf)]
            at = t * 288 + 16 + h * 128
            big[at : at + 128, :] = jnp.concatenate(parts, axis=0).T
        win[t * 64 : t * 64 + 64, :] = big[pl.ds(pl.multiple_of(t * 288 + ta * 32, 32), 64), :]
        for i in range(64):
            rev[t * 64 + i : t * 64 + i + 1, :] = win[t * 64 + 63 - i : t * 64 + 64 - i, :]
        win[256 + t * 64 : 320 + t * 64, :] = pltpu.roll(win[t * 64 : t * 64 + 64, :], 32, 1)
        rev[256 + t * 64 : 320 + t * 64, :] = pltpu.roll(rev[t * 64 : t * 64 + 64, :], 96, 1)
    near = (lax.broadcasted_iota(jnp.int32, (REACH, 128), 1) & 32) == 0
    for g in range(4):
        for f in range(7):
            t, odd = f // 2, f % 2
            low = 256 * odd + t * 64 + 44 - 8 * g
            high = 256 * (1 - odd) + t * 64 + 20 + 8 * g
            both = jnp.where(near, rev[low : low + REACH, :], win[high : high + REACH, :])
            out[g * ROWS + f * REACH : g * ROWS + (f + 1) * REACH, :] = both
        out[g * ROWS + 126 : g * ROWS + 128, :] = jnp.zeros((2, 128), F32)


def fold_kernel(recv, own, down, up, mix_d, mix_u):
    half0 = lanes() < 64

    def one(r):
        def at(i):
            return pl.ds(pl.multiple_of(i * ROWS + r * 8, 8), 8)

        v = exchange_bits([recv[at(gy), :] for gy in range(4)])
        for i in range(4):
            own[at(i), :] = v[i]
        mix_d[at(0), :] = jnp.where(half0, v[2], pltpu.roll(v[3], 64, 1))
        mix_u[at(0), :] = jnp.where(half0, pltpu.roll(v[3], 64, 1), v[2])

    def group(r, carry):
        for i in range(4):
            one(r * 4 + i)
        return carry

    lax.fori_loop(0, ROWS // 32, group, 0)
    for out, mix in ((down, mix_d), (up, mix_u)):
        for i in range(3):
            ref, at = (own, i * ROWS) if i < 2 else (mix, 0)
            for f in range(7):
                out[i * FAR + f * 8 : i * FAR + f * 8 + 8, :] = ref[at + f * REACH : at + f * REACH + 8, :]
                out[i * FAR + 56 + f : i * FAR + 57 + f, :] = ref[at + f * REACH + 8 : at + f * REACH + 9, :]
            out[i * FAR + 63 : i * FAR + 64, :] = jnp.zeros((1, 128), F32)


def main_kernel(pos_ref, stiff_tab, cond_tab, own, east, west, east2, west2, out, a_st, b_st, c_st, t0, t1, raw, co):
    lane = lanes()
    row = lax.broadcasted_iota(jnp.int32, (8, 128), 0)
    half0 = lane < 64
    near_z = (lane & 32) == 0
    y = lane & 31
    has_n, has_s = y < 31, y > 0
    zero = jnp.zeros((8, 128), F32)

    def swap_x(v):
        return pltpu.roll(v, 64, 1)

    def swap_z(v):
        return jnp.where(near_z, pltpu.roll(v, 96, 1), pltpu.roll(v, 32, 1))

    def tile(start):
        return pl.ds(pl.multiple_of(start, 8), 8)

    def spread(r, carry):
        def get(ref, i):
            return ref[tile(i * ROWS + r * 8), :]

        def place(xi, v):
            raw[pl.ds(r * (8 * PLANE) + xi, 8, stride=PLANE), :] = v

        for i in range(4):
            place(i, get(own, i))
            place(4 + i, swap_x(jnp.where(half0, get(east, 3 - i), get(west, 3 - i))))
            place(8 + i, jnp.where(half0, get(west, i), get(east, i)))
        for i in range(12, 24):
            place(i, zero)
        return carry

    lax.fori_loop(0, ROWS // 8, spread, 0)
    for q in range(8):

        def put_far(xi, v):
            if q < 7:
                raw[pl.ds(q * REACH * PLANE + xi, 8, stride=PLANE), :] = v
            else:
                raw[pl.ds(8 * PLANE + xi, 8, stride=REACH * PLANE), :] = v

        e = [east2[i * FAR + q * 8 : i * FAR + q * 8 + 8, :] for i in range(3)]
        w = [west2[i * FAR + q * 8 : i * FAR + q * 8 + 8, :] for i in range(3)]
        put_far(12, jnp.where(half0, w[2], e[2]))
        put_far(13, swap_x(jnp.where(half0, e[2], w[2])))
        for i in range(2):
            put_far(14 + i, swap_x(jnp.where(half0, e[1 - i], w[1 - i])))
            put_far(16 + i, jnp.where(half0, w[i], e[i]))

    x0, z0 = pos_ref[0], pos_ref[1]

    def coefficients(zi, carry):
        z = jnp.where(near_z, z0 + 3 - zi, z0 + 4 + zi)
        in_z = (z >= 0) & (z < 256)
        for b in range(3):
            xi = row + 8 * b
            x = jnp.where(half0, x0 + 3 - xi, x0 + 4 + xi)
            here = in_z & (x >= 0) & (x < 64)
            label = raw[tile((5 * REACH + zi) * PLANE + 8 * b), :]
            drain = raw[tile((6 * REACH + zi) * PLANE + 8 * b), :]
            stiff, cond = zero, zero
            for i in range(6):
                hit = label == float(i)
                stiff = jnp.where(hit, stiff_tab[i], stiff)
                cond = jnp.where(hit, cond_tab[i], cond)
            stiff = jnp.where(here, stiff, 0.0)
            fine_a = stiff * fine_dt
            coarse_a = stiff * (fine_dt * FINE)
            values = (
                fine_a,
                1.0 - 6.0 * fine_a,
                coarse_a,
                1.0 - 6.0 * coarse_a,
                jnp.where(here, 1.0 - drain, 0.0),
                jnp.where(here, cond, -1.0e30),
                jnp.where(here, 1.0, 0.0).astype(F32),
            )
            for i, value in enumerate(values):
                co[tile(i * FIELD + (zi + 1) * PLANE + 8 + 8 * b), :] = value
        return carry

    lax.fori_loop(0, REACH, coefficients, 0)

    sign_x = jnp.where(half0, -U_SCALE, U_SCALE).astype(F32)
    sign_z = jnp.where(near_z, -U_SCALE, U_SCALE).astype(F32)

    def where_of(slot, zi, b0=0):
        return pl.multiple_of(slot * SLOT + (zi + 1) * PLANE + 8 + 8 * b0, 8)

    def load(ref, at, f, off=0):
        return ref[pl.ds(at + (f * FIELD + off), 8), :]

    def coef(at, i, off):
        return co[pl.ds(at + (i * FIELD + off), 8), :]

    def put(ref, at, off, vals, k=None):
        for f in range(5):
            ref[pl.ds(at + (f * FIELD + off), 8), :] = vals[f]
        if k is not None:
            ref[pl.ds(at + (5 * FIELD + off), 8), :] = k

    def conduct(ca, off, psi):
        return jnp.exp2(coef(ca, 5, off) - psi)

    def begin(zi, carry):
        at, ca = where_of(0, zi), where_of(0, zi)
        for b in range(3):
            vals = [raw[tile((f * REACH + zi) * PLANE + 8 * b), :] for f in range(5)]
            vals[0] = vals[0] * sign_x
            vals[1] = vals[1] * U_SCALE
            vals[2] = vals[2] * sign_z
            vals[3] = vals[3] * P_SCALE
            vals[4] = (1.0 - vals[4]) * SHARP
            k = conduct(ca, 8 * b, vals[4])
            for ref in (a_st, t1):
                put(ref, at, 8 * b, vals, k)
        return carry

    lax.fori_loop(0, REACH, begin, 0)

    def north(v):
        return jnp.where(has_n, pltpu.roll(v, 127, 1), 0.0)

    def south(v):
        return jnp.where(has_s, pltpu.roll(v, 1, 1), 0.0)

    def advance(ref, slot, radius, fine, emit):
        inner = (radius + 1) // 2
        passes = jnp.where(radius > 12, 2, 1)

        near = [(d * PLANE + 8 * b, b) for d in range(2) for b in range(2)]
        far = [(d * PLANE, 0) for d in range(4)]

        def unit(at, ca, carry, tiles):
            carry = list(carry)
            for off, b in tiles:
                mid = {f: load(ref, at, f, off) for f in MOVED}
                e = {f: load(ref, at, f, off + 1) for f in MOVED}
                w = {f: load(ref, at, f, off - 1) for f in MOVED}
                i = {f: load(ref, at, f, off + PLANE) for f in MOVED}
                o = {f: load(ref, at, f, off - PLANE) for f in (0, 1, 2, 3)}
                n, s = {}, {}
                for j, f in enumerate(MOVED):
                    n[f] = north(mid[f])
                    s[f] = south(mid[f])
                p, k = mid[3], mid[5]
                face = (i[5] + k) * (i[3] - p)
                flux = face - carry[b]
                carry[b] = face
                for side in (e, w, n, s):
                    flux = flux + (side[5] + k) * (side[3] - p)
                dil = (e[0] - w[0]) + (n[1] - s[1]) + (i[2] - o[2])
                m = coef(ca, 6, off)
                grads = [e[3] - w[3], n[3] - s[3], i[3] - o[3]]
                gain = GAIN
                if not fine:
                    m = m * float(FINE)
                    grads[1] = grads[1] * float(FINE)
                    flux = flux * float(FINE)
                    gain = GAIN * FINE
                grads[0] = grads[0] * m
                grads[2] = grads[2] * m
                a = coef(ca, 0 if fine else 2, off)
                a6 = coef(ca, 1 if fine else 3, off)
                new = []
                for f in range(3):
                    around = (e[f] + w[f]) + (n[f] + s[f]) + (i[f] + o[f])
                    new.append(a * around + a6 * mid[f] - grads[f])
                new.append(coef(ca, 4, off) * (p + (flux - gain * dil)))
                psi = load(ref, at, 4, off)
                new.append(psi * (1.0 - (dil if fine else dil * float(FINE))))
                emit(at - slot * SLOT, ca, off, new)
            return tuple(carry)

        start = where_of(slot, 0)

        def ghost_x(f, zi):
            row0 = start + (f * FIELD + zi * PLANE)
            v = ref[pl.ds(row0, 8, stride=PLANE), :]
            ref[pl.ds(row0 - 1, 8, stride=PLANE), :] = swap_x(-v if f == 0 else v)

        def ghost_z(f, b):
            v = load(ref, start, f, 8 * b)
            v = swap_z(-v if f == 2 else v)
            ref[pl.ds(start + (f * FIELD + 8 * b - PLANE), 8), :] = v
            return v

        @pl.when(radius > 12)
        def _():
            for f in MOVED:
                ghost_z(f, 2)
                ghost_x(f, 10)

        def one_pass(j, c):
            b0 = passes - 1 - j
            at, ca = where_of(slot, 0, b0), where_of(0, 0, b0)
            for f in MOVED:
                ghost_x(f, 0)
                ghost_x(f, 8)
            for f in (0, 1, 2):
                for b in range(2):
                    ghost_z(f, b)
            carry = []
            for b in range(2):
                ghost_z(3, b)
                ghost_z(5, b)
            for b in range(2):
                k0, k1 = load(ref, at, 5, 8 * b - PLANE), load(ref, at, 5, 8 * b)
                p0, p1 = load(ref, at, 3, 8 * b - PLANE), load(ref, at, 3, 8 * b)
                carry.append((k0 + k1) * (p1 - p0))

            units = jnp.where(b0 == 0, inner, 2)

            def moved(u, carry, tiles=near):
                shift = u * (2 * PLANE)
                return unit(pl.multiple_of(at + shift, 8), pl.multiple_of(ca + shift, 8), carry, tiles)

            def two(u, carry):
                return moved(2 * u + 1, moved(2 * u, carry))

            carry = lax.fori_loop(0, units // 2, two, tuple(carry))

            @pl.when(units % 2 == 1)
            def _():
                moved(units, moved(units - 1, carry), far)

            @pl.when((units % 2 == 0) & (b0 == 0))
            def _():
                moved(units, carry, far)

            return c

        lax.fori_loop(0, passes, one_pass, 0)

    def slot_at(slot, at):
        return pl.multiple_of(slot * SLOT + at, 8)

    def plain(src, slot, radius, fine, *targets):
        def emit(at, ca, off, new):
            k = conduct(ca, off, new[4])
            for ref, to in targets:
                put(ref, slot_at(to, at), off, new, k)

        advance(src, slot, radius, fine, emit)

    def minus(src, slot, radius, sub, to):
        def emit(at, ca, off, new):
            old = slot_at(sub, at)
            put(c_st, slot_at(to, at), off, [new[f] - load(a_st, old, f, off) for f in range(5)])

        advance(src, slot, radius, True, emit)

    def plus(src, radius, cor, keep, *targets):
        def emit(at, ca, off, new):
            if keep is not None:
                put(a_st, slot_at(keep, at), off, new)
            if targets:
                old = slot_at(cor, at)
                vals = [new[f] + load(c_st, old, f, off) for f in range(5)]
                k = conduct(ca, off, vals[4])
                for ref, to in targets:
                    put(ref, slot_at(to, at), off, vals, k)

        advance(src, 0, radius, False, emit)

    def fine_all(source, base, start):
        def slab(j, carry):
            plain(source, base + j, start - j, True, (t0, 0))
            plain(t0, 0, start - 1 - j, True, (t1, 0))
            plain(t1, 0, start - 2 - j, True, (t0, 0))
            minus(t0, 0, start - 3 - j, j + 1, j)

            @pl.when(j == 0)
            def _():
                for zi in range(4):
                    put(b_st, where_of(0, zi), 0, [load(b_st, where_of(1, zi), f) for f in range(5)])

                def body(zi, carry):
                    at = where_of(0, zi)
                    for b in range(2):
                        off = 8 * b
                        vals = [load(a_st, slot_at(1, at), f, off) + load(c_st, at, f, off) for f in range(5)]
                        put(b_st, slot_at(1, at), off, vals, conduct(at, off, vals[4]))
                    return carry

                lax.fori_loop(0, start + 1, body, 0)

            return carry

        lax.fori_loop(0, 7, slab, 0)

    def restart():
        def step(i, carry):
            for j in range(9):
                at = i * 72 + 8 * j
                t1[tile(at), :] = b_st[tile(SLOT + at), :]
            return carry

        lax.fori_loop(0, SLOT // 72, step, 0)

    def chain0(i, carry):
        k = 2 * i
        plain(t1, 0, 13 - k, False, (t0, 0), (a_st, k + 1))
        plain(t0, 0, 12 - k, False, (t1, 0), (a_st, k + 2))
        return carry

    lax.fori_loop(0, 3, chain0, 0)
    plain(t1, 0, jnp.int32(4), False, (a_st, 7))
    fine_all(a_st, 0, 13)
    restart()

    def chain1(i, carry):
        k = 2 * i + 1
        plus(t1, 10 - k, k, k, (t0, 0), (b_st, k + 1))
        plus(t0, 9 - k, k + 1, k + 1, (t1, 0), (b_st, k + 2))
        return carry

    lax.fori_loop(0, 3, chain1, 0)
    plus(t1, jnp.int32(0), None, 7)
    fine_all(b_st, 1, 9)
    restart()

    def chain2(i, carry):
        k = 2 * i + 2
        plus(t1, 7 - k, k - 1, None, (t0, 0), (b_st, k))
        plus(t0, 6 - k, k, None, (t1, 0), (b_st, k + 1))
        return carry

    lax.fori_loop(0, 3, chain2, 0)

    unsign_x = jnp.where(half0, -1.0 / U_SCALE, 1.0 / U_SCALE).astype(F32)
    unsign_z = jnp.where(near_z, -1.0 / U_SCALE, 1.0 / U_SCALE).astype(F32)
    for f in range(5):
        for zi in range(4):
            v = []
            for xi in range(4):
                e = b_st[pl.ds(f * FIELD + (zi + 1) * PLANE + 8 + xi, 8, stride=SLOT), :]
                if f == 4:
                    e = 1.0 - e * (1.0 / SHARP)
                else:
                    e = e * (unsign_x, 1.0 / U_SCALE, unsign_z, 1.0 / P_SCALE)[f]
                v.append(e)
            v = exchange_bits(v)
            for gy in range(4):
                out[pl.ds(gy * 20 + f * 4 + zi, 8, stride=80), :] = v[gy]


def unpack_kernel(recv, out, rows):
    near_z = (lanes() & 32) == 0
    for t in range(3):
        for zi in range(4):
            for g in range(4):
                one = recv[pl.ds(g * 160 + 2 * t * 4 + zi, 8, stride=20), :]
                two = recv[pl.ds(g * 160 + min(2 * t + 1, 4) * 4 + zi, 8, stride=20), :]
                low = jnp.where(near_z, one, pltpu.roll(two, 32, 1))
                high = jnp.where(near_z, pltpu.roll(one, 96, 1), two)
                rows[pl.ds(t * 256 + g * 64 + 3 - zi, 8, stride=8), :] = low
                rows[pl.ds(t * 256 + g * 64 + 4 + zi, 8, stride=8), :] = high
        for h in range(2):
            block = rows[t * 256 + h * 128 : t * 256 + (h + 1) * 128, :].T
            for i in range(1 if t == 2 else 2):
                for xf in range(2):
                    for xi in range(4):
                        at = ((2 * t + i) * 8 + (4 + xi if xf else 3 - xi)) * 8
                        source = xf * 64 + i * 32 + xi * 8
                        out[at : at + 8, h * 128 : (h + 1) * 128] = block[source : source + 8, :]


def vmem():
    return pl.BlockSpec(memory_space=pltpu.VMEM)


def smem():
    return pl.BlockSpec(memory_space=pltpu.SMEM)


def scratch(rows):
    return pltpu.VMEM((rows, 128), F32)


def shaped(rows, width=128):
    return jax.ShapeDtypeStruct((rows, width), F32)


def pack(ta, *fields):
    return pl.pallas_call(
        pack_kernel,
        out_shape=shaped(4 * ROWS),
        in_specs=[smem()] + [vmem()] * 5,
        out_specs=vmem(),
        scratch_shapes=[scratch(896), scratch(1152), scratch(512), scratch(512)],
        interpret=INTERPRET,
        name="pack",
    )(ta, *fields)


def fold(recv):
    return pl.pallas_call(
        fold_kernel,
        out_shape=(shaped(4 * ROWS), shaped(3 * FAR), shaped(3 * FAR)),
        in_specs=[vmem()],
        out_specs=(vmem(), vmem(), vmem()),
        scratch_shapes=[scratch(ROWS), scratch(ROWS)],
        compiler_params=pltpu.CompilerParams(vmem_limit_bytes=8 << 20),
        interpret=INTERPRET,
        name="fold",
    )(recv)


def compute(pos, stiff_table, perm_table, *blocks):
    cond_table = jnp.log2(perm_table) + (math.log2(0.5 * fine_dt) + SHARP * (1.0 - porosity_ref))
    return pl.pallas_call(
        main_kernel,
        out_shape=shaped(32 * 20),
        in_specs=[smem(), smem(), smem()] + [vmem()] * 5,
        out_specs=vmem(),
        scratch_shapes=[
            scratch(8 * SLOT + PAD),
            scratch(8 * SLOT + PAD),
            scratch(7 * SLOT + PAD),
            scratch(SLOT + PAD),
            scratch(SLOT + PAD),
            scratch(ROWS * PLANE + 256),
            scratch(7 * FIELD + PAD),
        ],
        compiler_params=pltpu.CompilerParams(vmem_limit_bytes=42 << 20),
        interpret=INTERPRET,
        name="parareal",
    )(pos, stiff_table, cond_table, *blocks)


def unpack(recv):
    return pl.pallas_call(
        unpack_kernel,
        out_shape=shaped(320, 256),
        in_specs=[vmem()],
        out_specs=vmem(),
        scratch_shapes=[scratch(768)],
        compiler_params=pltpu.CompilerParams(vmem_limit_bytes=8 << 20),
        interpret=INTERPRET,
        name="unpack",
    )(recv)


def shards(displacement, pressure, porosity, labels, ventricle_mask, stiff_table, perm_table):
    ta, gx, gy = (lax.axis_index(name).astype(jnp.int32) for name in ("ta", "gx", "gy"))
    flat = lambda a: a.reshape(a.shape[:-3] + (64, 256))
    sent = pack(
        ta.reshape(1), flat(displacement), flat(pressure), flat(porosity), flat(labels), flat(ventricle_mask)
    )
    got = lax.all_to_all(sent.reshape(4, ROWS, 128), "gy", 0, 0, tiled=True)
    own, down, up = fold(got.reshape(4 * ROWS, 128))

    def from_side(value, by):
        pairs = [(i, i - by) for i in range(8) if 0 <= i - by < 8]
        return lax.ppermute(value, "gx", pairs)

    blocks = (own, from_side(own, 1), from_side(own, -1), from_side(down, 2), from_side(up, -2))
    ends = compute(jnp.stack([gx * 8, ta * 32 + gy * 8]), stiff_table, perm_table, *blocks)
    mine = lax.all_to_all(ends.reshape(32, 5, 4, 128), ("ta", "gy"), 0, 0, tiled=True)
    return unpack(mine.reshape(32 * 20, 128)).reshape(1, 5, 8, 8, 256)


def solution(mesh):
    placed = (
        P(None, "gx", "gy", None),
        P("gx", "gy", None),
        P("gx", "gy", None),
        P("gx", "gy", None),
        P("gx", "gy", None),
        P(),
        P(),
    )
    return jax.shard_map(
        shards,
        mesh=mesh,
        in_specs=placed,
        out_specs=P("ta", None, "gx", "gy", None),
        check_vma=False,
    )
```
